512 devices in a mesh: beam: 32 (over y, x), trans: 16 (over z, core).
Axes of the slice: x: 4, y: 8, z: 8, core: 2. Of those that a mesh axis runs over, the one named last changes fastest.
Arguments:
- field_in: float32 [2, 128, 256, 256], P(None, 'beam', 'trans'), may hold values from -4 to 4
- phases: float32 [128, 4096], P('beam'), may hold values from -3.140625 to 3.140625
- energy: float32 [128, 4096], P('beam'), may hold values from -3 to 3
- row_cell: int32 [128, 4096], P('beam'), may hold values from 32 to 223
- col_cell: int32 [128, 4096], P('beam'), may hold values from 32 to 223
- weight: int32 [128, 4096], P('beam'), may hold values from 1 to 15
- charge: int32 [128], P('beam'), may hold values from 256 to 1024
- pole_rate: float32 [8], replicated, may hold values from 0.001953125 to 0.5
- pole_freq: float32 [8], replicated, may hold values from 0 to 0.3
- pole_amp: float32 [8], replicated, may hold values from -3 to 3
Outputs:
- field_out: float32 [2, 128, 256, 256], P(None, 'beam', 'trans')
- phase_out: float32 [128, 4096], P('beam')
- energy_out: float32 [128, 4096], P('beam')
The draws below stay inside these ranges and needn't reach their ends.
All inputs are finite; a program needn't handle non-finite values.
Results may differ from the reference program's by a relative error of at most 0.00042.
Values sent between devices are 32-bit elements; how exact they have to be, the bound alone decides.
No kernel may reach another device: no remote copies, remote signals or barrier semaphores. Data moves between devices by JAX's collectives and lax.ppermute only.
A program may use at most 64 MiB of HBM per device.

```python
import math
import jax
import jax.numpy as jnp
from jax import lax

GRID = 256
NPART = 4096
POLES = 8
PERIODS = 2
SLICES = 128


def with_ends(values, key, least, largest):
    dims = values.shape
    spot = [jax.random.randint(jax.random.fold_in(key, axis), (), 0, dims[axis]) for axis in range(len(dims))]
    values = values.at[tuple(spot)].set(least)
    longest = dims.index(max(dims))
    spot[longest] = (spot[longest] + 1) % dims[longest]
    return values.at[tuple(spot)].set(largest)


def block_scale(own_key, shape, shards, least, top_value):
    loudness, own = 1.0, jax.random.fold_in(own_key, 6)
    for dim, parts in shards:
        steps = jnp.exp(jax.random.uniform(jax.random.fold_in(own, dim), (parts,), jnp.float32, least / len(shards), top_value / len(shards)))
        loudness = loudness * jnp.repeat(steps, shape[dim] // parts).reshape([-1 if axis == dim else 1 for axis in range(len(shape))])
    return loudness


def scatter_about(rng, shape, spread, reach, split=(), held_as=jnp.bfloat16):
    factor_of = block_scale(rng, shape, split, -0.22, 0.18) if split else 1.0
    drawn = jax.random.normal(rng, shape, jnp.float32) * spread * factor_of
    return jnp.minimum(jnp.maximum(drawn, -reach), reach).astype(held_as)


def setup_inputs(seed: int = 0) -> dict:
    splits = jax.random.split(jax.random.key(seed), 11)
    field_in = scatter_about(splits[0], (2, SLICES, GRID, GRID), 0.5, 4.0, ((1, 32), (2, 16)), jnp.float32)
    phases = jnp.clip(jax.random.uniform(splits[1], (SLICES, NPART), jnp.float32, -3.140625, 3.140625), -3.140625, 3.140625)
    energy = scatter_about(splits[2], (SLICES, NPART), 0.5, 3.0, ((0, 32),), jnp.float32)
    row_cell = with_ends(jax.random.randint(splits[3], (SLICES, NPART), GRID // 8, GRID - GRID // 8), jax.random.fold_in(splits[3], 1), GRID // 8, (GRID - GRID // 8) - 1).astype(jnp.int32)
    col_cell = with_ends(jax.random.randint(splits[4], (SLICES, NPART), GRID // 8, GRID - GRID // 8), jax.random.fold_in(splits[4], 1), GRID // 8, (GRID - GRID // 8) - 1).astype(jnp.int32)
    weight = with_ends(jax.random.randint(splits[5], (SLICES, NPART), 1, 16), jax.random.fold_in(splits[5], 1), 1, 15).astype(jnp.int32)
    charge = with_ends(jax.random.randint(splits[6], (SLICES,), 256, 1025), jax.random.fold_in(splits[6], 1), 256, 1024).astype(jnp.int32)
    pole_rate = jnp.clip(jnp.exp(jax.random.uniform(splits[7], (POLES,), jnp.float32, math.log(0.001953125), math.log(0.5))), 0.001953125, 0.5)
    pole_freq = jnp.clip(jax.random.uniform(splits[8], (POLES,), jnp.float32, 0.0, 0.3), 0.0, 0.3)
    pole_amp = scatter_about(splits[9], (POLES,), 0.5, 3.0, (), jnp.float32)
    return dict(field_in=field_in, phases=phases, energy=energy, row_cell=row_cell, col_cell=col_cell, weight=weight, charge=charge, pole_rate=pole_rate, pole_freq=pole_freq, pole_amp=pole_amp)


diffraction = 20.0
kick_gain = 0.5
deposit_gain = 0.05
wake_gain = 3.0
charge_unit = 1024.0


def wake_profile(charge_norm, pole_rate, pole_freq, pole_amp):
    damping = jnp.exp(-pole_rate)
    step_re = damping * jnp.cos(pole_freq)
    step_im = damping * jnp.sin(pole_freq)

    def advance(state, amount):
        state_re, state_im = state
        loaded = state_re + amount
        advanced = (step_re * loaded - step_im * state_im, step_im * loaded + step_re * state_im)
        return advanced, state_re

    initial = (jnp.zeros_like(pole_rate), jnp.zeros_like(pole_rate))
    ending, history = lax.scan(advance, initial, charge_norm)
    summed = jnp.sum(pole_amp[None, :] * (history + 0.5 * charge_norm[:, None]), axis=1)
    return (wake_gain / SLICES) * summed


def reference(field_in, phases, energy, row_cell, col_cell, weight, charge, pole_rate, pole_freq, pole_amp):
    charge_norm = charge.astype(jnp.float32) / charge_unit
    wake_kick = wake_profile(charge_norm, pole_rate, pole_freq, pole_amp)
    freq_index = jnp.arange(GRID, dtype=jnp.int32)
    centred = ((freq_index + GRID // 2) % GRID - GRID // 2).astype(jnp.float32) / GRID
    kernel_phase = diffraction * (centred[:, None] ** 2 + centred[None, :] ** 2)
    propagator = jnp.cos(kernel_phase) - 1j * jnp.sin(kernel_phase)
    slice_ids = jnp.arange(SLICES, dtype=jnp.int32)[:, None]
    weights = weight.astype(jnp.float32)
    wavefront = field_in[0] + 1j * field_in[1]
    angles = phases
    energies = energy
    for period in range(PERIODS):
        probed = wavefront[slice_ids, row_cell, col_cell]
        energies = energies - kick_gain * (jnp.real(probed) * jnp.cos(angles) - jnp.imag(probed) * jnp.sin(angles)) - wake_kick[:, None]
        angles = angles + energies
        bunch_re = lax.optimization_barrier((weights * jnp.cos(angles)).astype(jnp.bfloat16)).astype(jnp.float32)
        bunch_im = lax.optimization_barrier((-weights * jnp.sin(angles)).astype(jnp.bfloat16)).astype(jnp.float32)
        empty = jnp.zeros((SLICES, GRID, GRID), jnp.float32)
        grid_re = empty.at[slice_ids, row_cell, col_cell].add(bunch_re)
        grid_im = empty.at[slice_ids, row_cell, col_cell].add(bunch_im)
        wavefront = wavefront + (deposit_gain * charge_norm)[:, None, None] * (grid_re + 1j * grid_im)
        spectrum = jnp.fft.fft2(wavefront, norm="ortho") * propagator
        wavefront = jnp.fft.ifft2(spectrum, norm="ortho")
        wavefront = jnp.concatenate([jnp.zeros_like(wavefront[:1]), wavefront[:-1]], axis=0)
    field_out = jnp.stack([jnp.real(wavefront), jnp.imag(wavefront)])
    return field_out, angles, energies
```

```python
import functools
import math

import jax
import jax.numpy as jnp
import numpy as np
from jax import lax
from jax.experimental import pallas as pl
from jax.experimental.pallas import tpu as pltpu
from jax.sharding import PartitionSpec as P

diffraction = 20.0
kick_gain = 0.5
deposit_gain = 0.05
wake_gain = 3.0
charge_unit = 1024.0

GRID = 256
SLICES = 128
NPART = 4096
BEAM = 32
TRANS = 16
LOW, HIGH = 32, 224
SPAN = HIGH - LOW
ROWS, WIDE = 8, 512
JOINT = ("beam", "trans")
QUADS = [[4 * r + c for c in range(4)] for r in range(4)]

f32 = jnp.float32
bf16 = jnp.bfloat16


def propagation_table():
    n = np.arange(GRID)
    centred = ((n + GRID // 2) % GRID - GRID // 2) / GRID
    k = np.exp(-1j * diffraction * centred**2)
    h = np.fft.ifft(k)
    a = h[(n[:, None] - n[None, :]) % GRID]
    parts = np.stack([a.real, a.imag]).astype(np.float32)
    high = parts.astype(jnp.bfloat16)
    low = (parts - high.astype(np.float32)).astype(jnp.bfloat16)
    return high, low


def moved(fn):
    out = []
    for b in range(BEAM):
        for t in range(TRANS):
            b2, t2 = fn(b, t)
            out.append((b * TRANS + t, (b2 % BEAM) * TRANS + t2))
    return out


FROM_EVEN = moved(lambda b, t: (b - 2 * t, t))
FROM_ODD = moved(lambda b, t: (b - 2 * t - 1, t))
TO_PREVIOUS = moved(lambda b, t: ((4 * b + t % 4 - 1) // 4, t // 4 * 4 + (t % 4 - 1) % 4))
NEXT_BEAM = [(b, (b + 1) % BEAM) for b in range(BEAM)]
NEXT_BEAM_PAIR = [
    (b * TRANS + t, (b + 1) % BEAM * TRANS + t)
    for b in range(BEAM)
    for t in range(TRANS)
    if t % 4 < 2
]


def split(x):
    high = x.astype(bf16)
    return high, (x - high.astype(f32)).astype(bf16)


def dot(a, b):
    return jnp.dot(a, b, preferred_element_type=f32)


def times_right(xr, xi, high, low):
    m = xr.shape[0]
    xh, xl = split(jnp.concatenate([xr, xi], axis=0))
    pr = dot(xh, high[0]) + dot(xl, high[0]) + dot(xh, low[0])
    pi = dot(xh, high[1]) + dot(xl, high[1]) + dot(xh, low[1])
    return pr[:m] - pi[m:], pi[:m] + pr[m:]


def times_left(ah, al, xr, xi):
    m = ah.shape[0] // 2
    rh, rl = split(xr)
    ih, il = split(xi)
    qr = dot(ah, rh) + dot(al, rh) + dot(ah, rl)
    qi = dot(ah, ih) + dot(al, ih) + dot(ah, il)
    return qr[:m] - qi[m:], qr[m:] + qi[:m]


def iota_rows(first, count):
    return lax.broadcasted_iota(jnp.int32, (count, WIDE), 0).astype(f32) + float(first)


def hot(values, rows_bf):
    return jnp.where(rows_bf == values.astype(bf16), jnp.ones((), bf16), jnp.zeros((), bf16))


def probe(fr, fi, rows, cols, out_re, out_im):
    high, low = split(jnp.concatenate([fr[LOW:HIGH], fi[LOW:HIGH]], axis=0))
    col_iota = iota_rows(0, GRID).astype(bf16)
    row_iota = iota_rows(LOW, SPAN)
    for q in range(ROWS):
        col_hot = hot(cols[q : q + 1], col_iota)
        found = dot(high, col_hot) + dot(low, col_hot)
        mask = row_iota == rows[q : q + 1]
        out_re[q : q + 1, :] = jnp.sum(jnp.where(mask, found[:SPAN], 0.0), axis=0, keepdims=True)
        out_im[q : q + 1, :] = jnp.sum(jnp.where(mask, found[SPAN:], 0.0), axis=0, keepdims=True)


def deposit(angles, weights, rows, cols):
    v = (weights * jnp.cos(angles)).astype(bf16)
    u = (-weights * jnp.sin(angles)).astype(bf16)
    col_iota = iota_rows(0, GRID).astype(bf16)
    row_iota = iota_rows(LOW, SPAN).astype(bf16)
    zero = jnp.zeros((), bf16)
    total = jnp.zeros((2 * SPAN, GRID), f32)
    for q in range(ROWS):
        col_hot = hot(cols[q : q + 1], col_iota)
        mask = row_iota == rows[q : q + 1].astype(bf16)
        left = jnp.concatenate(
            [jnp.where(mask, v[q : q + 1], zero), jnp.where(mask, u[q : q + 1], zero)], axis=0
        )
        total = total + lax.dot_general(
            left, col_hot, (((1,), (1,)), ((), ())), preferred_element_type=f32
        )
    return total[:SPAN], total[SPAN:]


def deposited(field, change, strength):
    return jnp.concatenate(
        [field[:LOW], field[LOW:HIGH] + strength * change, field[HIGH:]], axis=0
    )


def place():
    t = lax.axis_index("trans")
    return lax.axis_index("beam"), t, t % 4, t // 4


def prep_body(field, phases, energy, row, col, weight, charge, field_send, send, own, charges):
    _, _, c, _ = place()
    field_send[...] = field[:, 2:4]
    one, two = jnp.where(c == 0, 2, 3), 3
    own_one, own_two = jnp.maximum(c - 2, 0), jnp.maximum(c - 1, 0)

    def pick(ref, index, target, slot):
        line = ref[pl.ds(index, 1), :].astype(f32)
        for q in range(ROWS):
            target[slot, q : q + 1, :] = line[:, q * WIDE : (q + 1) * WIDE]

    for slot, ref in enumerate((phases, energy, row, col, weight)):
        pick(ref, one, send, slot)
        pick(ref, own_one, own, slot)
    for slot, ref in enumerate((row, col, weight)):
        pick(ref, two, send, 5 + slot)
        pick(ref, own_two, own, 5 + slot)
    lane = lax.broadcasted_iota(jnp.int32, (8, 128), 1) % 4
    line = jnp.zeros((8, 128), f32)
    for k in range(4):
        line = jnp.where(lane == k, charge[k].astype(f32) / charge_unit, line)
    charges[...] = line


def pack_body(field, shifted, even, odd, out):
    _, t, _, _ = place()
    lane = lax.broadcasted_iota(jnp.int32, (8, 128), 1) // 4
    top = lax.broadcasted_iota(jnp.int32, (8, 128), 0) == 0
    line = jnp.where(lane == 2 * t, even[...], jnp.where(lane == 2 * t + 1, odd[...], 0.0))
    line = jnp.where(top, line, 0.0)
    for c in range(4):
        for part in range(2):
            piece = shifted[part, c] if c < 2 else field[part, c - 2]
            for half in range(2):
                at = (part * 2 + half) * 16
                for r in range(4):
                    out[4 * r + c, at : at + 16, :] = piece[:, half * 128 : (half + 1) * 128]
    for t2 in range(TRANS):
        out[t2, 64:72, :] = line


def whole_field(x, part):
    halves = [
        x[:, (part * 2 + half) * 16 : (part * 2 + half + 1) * 16, :].reshape(GRID, 128)
        for half in range(2)
    ]
    return jnp.concatenate(halves, axis=1)


def chosen(own, received, slot, from_received):
    return jnp.where(from_received, received[slot], own[slot])


def first_body(x, own, received, rate, freq, amp, states, extra, re, im):
    b, _, c, _ = place()
    g = 4 * b + c
    take = lambda slot: chosen(own, received, slot, c < 2)
    fr, fi = whole_field(x, 0), whole_field(x, 1)
    probe(fr, fi, take(2), take(3), re, im)
    charges = jnp.sum(x[:, 64:72, :], axis=0)
    charges = jnp.sum(charges, axis=0, keepdims=True)
    source = (4 * b + lax.broadcasted_iota(jnp.int32, (8, 128), 1)) % SLICES
    pole = lax.broadcasted_iota(jnp.int32, (8, 128), 0)
    rates, freqs, amps = (jnp.zeros((8, 128), f32) for _ in range(3))
    for k in range(8):
        rates = jnp.where(pole == k, rate[k], rates)
        freqs = jnp.where(pole == k, freq[k], freqs)
        amps = jnp.where(pole == k, amp[k], amps)

    def total(value):
        return jnp.sum(jnp.sum(value, axis=0, keepdims=True), axis=1, keepdims=True)

    wakes, norms = [], []
    for back in (2, 1):
        s = (g + SLICES - back) % SLICES
        steps = jnp.maximum(s - source, 0).astype(f32)
        power = jnp.exp(-rates * steps) * jnp.cos(freqs * steps)
        reach = jnp.where(source < s, power, jnp.where(source == s, 0.5, 0.0))
        wakes.append(wake_gain / SLICES * total(amps * reach * charges))
        norms.append(total(jnp.where((source == s) & (pole == 0), charges, 0.0)))
    for k, value in enumerate((*wakes, *norms)):
        extra[k] = jnp.broadcast_to(value, (8, 128))
    angles = take(0)
    energies = (
        take(1) - kick_gain * (re[...] * jnp.cos(angles) - im[...] * jnp.sin(angles)) - wakes[0]
    )
    states[0] = angles + energies
    states[1] = energies


def second_body(x, states, own, received, extra, high, low, field, re, im):
    b, _, c, _ = place()
    take = lambda slot: chosen(own, received, slot, c < 2)
    br, bi = deposit(states[0], take(4), take(2), take(3))
    strength = deposit_gain * extra[2, 0:1, 0:1]
    fr = deposited(whole_field(x, 0), br, strength)
    fi = deposited(whole_field(x, 1), bi, strength)
    fr, fi = times_right(fr, fi, high, low)
    fr, fi = times_left(high[...].reshape(2 * GRID, GRID), low[...].reshape(2 * GRID, GRID), fr, fi)
    first = (b == 0) & (c == 1)
    fr = jnp.where(first, 0.0, fr)
    fi = jnp.where(first, 0.0, fi)
    field[0] = fr
    field[1] = fi
    take = lambda slot: chosen(own, received, slot, c < 1)
    probe(fr, fi, take(5), take(6), re, im)


def third_body(states, extra, re, im, out):
    angles = states[0]
    energies = (
        states[1]
        - kick_gain * (re[...] * jnp.cos(angles) - im[...] * jnp.sin(angles))
        - extra[1, 0:1, 0:1]
    )
    out[0] = angles + energies
    out[1] = energies


def fourth_body(field, states, own, received, extra, high, low, out):
    b, _, c, r = place()
    take = lambda slot: chosen(own, received, slot, c < 1)
    br, bi = deposit(states[0], take(7), take(5), take(6))
    strength = deposit_gain * extra[3, 0:1, 0:1]
    fr = deposited(field[0], br, strength)
    fi = deposited(field[1], bi, strength)
    at = pl.multiple_of(r * 64, 64)
    ah = jnp.concatenate([high[0, pl.ds(at, 64), :], high[1, pl.ds(at, 64), :]], axis=0)
    al = jnp.concatenate([low[0, pl.ds(at, 64), :], low[1, pl.ds(at, 64), :]], axis=0)
    fr, fi = times_left(ah, al, fr, fi)
    fr, fi = times_right(fr, fi, high, low)
    empty = (b == 0) & (c == 0)
    for part, value in enumerate((fr, fi)):
        value = jnp.where(empty, 0.0, value)
        for j in range(4):
            out[j, part * 16 : part * 16 + 16, :] = value[16 * j : 16 * j + 16]


def last_body(x, field, phase, energy):
    for c in range(4):
        for part in range(2):
            field[part, c] = x[c, part * 16 : part * 16 + 16, :]
        for k, target in enumerate((phase, energy)):
            for half in range(2):
                at = 32 + (k * 2 + half) * 8
                piece = x[c, at : at + 8, :]
                for q in range(ROWS):
                    begin = q * WIDE + half * 256
                    target[c : c + 1, begin : begin + 256] = piece[q : q + 1]


def call(body, outs, *args, scalars=(), scratch=()):
    specs = [
        pl.BlockSpec(memory_space=pltpu.SMEM if k in scalars else pltpu.VMEM)
        for k in range(len(args))
    ]
    return pl.pallas_call(
        body,
        out_shape=[jax.ShapeDtypeStruct(shape, f32) for shape in outs],
        in_specs=specs,
        out_specs=[pl.BlockSpec(memory_space=pltpu.VMEM) for _ in outs],
        scratch_shapes=list(scratch),
    )(*args)


def shards(
    field_in, phases, energy, row_cell, col_cell, weight, charge, pole_rate, pole_freq, pole_amp
):
    high, low = propagation_table()
    high, low = jnp.asarray(high), jnp.asarray(low)
    kept = (8, ROWS, WIDE)
    state_shape = (2, ROWS, WIDE)
    line = (ROWS, WIDE)
    field_send, send, own, charges = call(
        prep_body,
        [(2, 2, 16, GRID), kept, kept, (8, 128)],
        field_in, phases, energy, row_cell, col_cell, weight, charge,
        scalars=(6,),
    )
    shifted = lax.ppermute(field_send, "beam", NEXT_BEAM)
    even = lax.ppermute(charges, JOINT, FROM_EVEN)
    odd = lax.ppermute(charges, JOINT, FROM_ODD)
    received = lax.ppermute(send, JOINT, NEXT_BEAM_PAIR)
    (packed,) = call(pack_body, [(TRANS, 72, 128)], field_in, shifted, even, odd)
    x = lax.all_to_all(packed, "trans", 0, 0, tiled=True)
    states, extra, _, _ = call(
        first_body,
        [state_shape, (4, 8, 128), line, line],
        x, own, received, pole_rate, pole_freq, pole_amp,
        scalars=(3, 4, 5),
    )
    following = lax.ppermute(states, JOINT, TO_PREVIOUS)
    field, re, im = call(
        second_body,
        [(2, GRID, GRID), line, line],
        x, states, own, received, extra, high, low,
    )
    (final,) = call(third_body, [state_shape], following, extra, re, im)
    home = lax.ppermute(final, JOINT, TO_PREVIOUS)
    (bands,) = call(
        fourth_body, [(4, 32, GRID)], field, final, own, received, extra, high, low
    )
    home = jnp.concatenate([home[..., :256], home[..., 256:]], axis=1).reshape(32, 256)
    both = jnp.concatenate([bands, jnp.broadcast_to(home[None], (4, 32, 256))], axis=1)
    y = lax.all_to_all(both, "trans", 0, 0, tiled=True, axis_index_groups=QUADS)
    return tuple(
        call(last_body, [(2, 4, 16, GRID), (4, NPART), (4, NPART)], y)
    )


def solution(mesh):
    placed = (
        P(None, "beam", "trans", None),
        P("beam", None),
        P("beam", None),
        P("beam", None),
        P("beam", None),
        P("beam", None),
        P("beam"),
        P(),
        P(),
        P(),
    )
    return jax.shard_map(
        shards,
        mesh=mesh,
        in_specs=placed,
        out_specs=(P(None, "beam", "trans", None), P("beam", None), P("beam", None)),
        check_vma=False,
    )
```

```python
import functools
import math

import jax
import jax.numpy as jnp
import numpy as np
from jax import lax
from jax.experimental import pallas as pl
from jax.experimental.pallas import tpu as pltpu
from jax.sharding import PartitionSpec as P

diffraction = 20.0
kick_gain = 0.5
deposit_gain = 0.05
wake_gain = 3.0
charge_unit = 1024.0

GRID = 256
SLICES = 128
NPART = 4096
BEAM = 32
TRANS = 16
LOW, HIGH = 32, 224
SPAN = HIGH - LOW
ROWS, WIDE = 8, 512
JOINT = ("beam", "trans")
QUADS = [[4 * r + c for c in range(4)] for r in range(4)]

f32 = jnp.float32
bf16 = jnp.bfloat16


def propagation_table():
    n = np.arange(GRID)
    centred = ((n + GRID // 2) % GRID - GRID // 2) / GRID
    k = np.exp(-1j * diffraction * centred**2)
    h = np.fft.ifft(k)
    a = h[(n[:, None] - n[None, :]) % GRID]
    parts = np.stack([a.real, a.imag]).astype(np.float32)
    high = parts.astype(jnp.bfloat16)
    low = (parts - high.astype(np.float32)).astype(jnp.bfloat16)
    return high, low


def moved(fn):
    out = []
    for b in range(BEAM):
        for t in range(TRANS):
            b2, t2 = fn(b, t)
            out.append((b * TRANS + t, (b2 % BEAM) * TRANS + t2))
    return out


SPREAD = (
    (1, 4, 5), (3, 8, 11), (12, 20, 24), (7, 27, 28), (9, 16, 25), (2, 21, 23),
    (14, 19, 29), (15, 17, 30), (13, 18, 31), (6, 26, 28), (10, 22, 28),
)
FOURS = [
    [m * TRANS + t for m in group]
    for t in range(TRANS)
    for group in sorted({tuple(sorted([b, *(b ^ v for v in SPREAD[t % 11])])) for b in range(BEAM)})
]
TO_PREVIOUS = moved(lambda b, t: ((4 * b + t % 4 - 1) // 4, t // 4 * 4 + (t % 4 - 1) % 4))
NEXT_BEAM = [(b, (b + 1) % BEAM) for b in range(BEAM)]
PAIR_TO_NEXT = [
    (b * TRANS + t, (b + 1) % BEAM * TRANS + t)
    for b in range(BEAM)
    for t in range(TRANS)
    if t % 4 < 2
]


def split(x):
    high = x.astype(bf16)
    return high, (x - high.astype(f32)).astype(bf16)


def dot(a, b):
    return jnp.dot(a, b, preferred_element_type=f32)


def times_right(xr, xi, high, low):
    m = xr.shape[0]
    xh, xl = split(jnp.concatenate([xr, xi], axis=0))
    pr = dot(xh, high[0]) + dot(xl, high[0]) + dot(xh, low[0])
    pi = dot(xh, high[1]) + dot(xl, high[1]) + dot(xh, low[1])
    return pr[:m] - pi[m:], pi[:m] + pr[m:]


def times_left(ah, al, xr, xi):
    m = ah.shape[0] // 2
    rh, rl = split(xr)
    ih, il = split(xi)
    qr = dot(ah, rh) + dot(al, rh) + dot(ah, rl)
    qi = dot(ah, ih) + dot(al, ih) + dot(ah, il)
    return qr[:m] - qi[m:], qr[m:] + qi[:m]


def iota_rows(first, count):
    return lax.broadcasted_iota(jnp.int32, (count, WIDE), 0).astype(f32) + float(first)


def hot(values, rows_bf):
    return jnp.where(rows_bf == values.astype(bf16), jnp.ones((), bf16), jnp.zeros((), bf16))


def probe(fr, fi, rows, cols, out_re, out_im):
    high, low = split(jnp.concatenate([fr[LOW:HIGH], fi[LOW:HIGH]], axis=0))
    col_iota = iota_rows(0, GRID).astype(bf16)
    row_iota = iota_rows(LOW, SPAN)
    for q in range(ROWS):
        col_hot = hot(cols[q : q + 1], col_iota)
        found = dot(high, col_hot) + dot(low, col_hot)
        mask = row_iota == rows[q : q + 1]
        out_re[q : q + 1, :] = jnp.sum(jnp.where(mask, found[:SPAN], 0.0), axis=0, keepdims=True)
        out_im[q : q + 1, :] = jnp.sum(jnp.where(mask, found[SPAN:], 0.0), axis=0, keepdims=True)


def deposit(angles, weights, rows, cols):
    v = (weights * jnp.cos(angles)).astype(bf16)
    u = (-weights * jnp.sin(angles)).astype(bf16)
    col_iota = iota_rows(0, GRID).astype(bf16)
    row_iota = iota_rows(LOW, SPAN).astype(bf16)
    zero = jnp.zeros((), bf16)
    total = jnp.zeros((2 * SPAN, GRID), f32)
    for q in range(ROWS):
        col_hot = hot(cols[q : q + 1], col_iota)
        mask = row_iota == rows[q : q + 1].astype(bf16)
        left = jnp.concatenate(
            [jnp.where(mask, v[q : q + 1], zero), jnp.where(mask, u[q : q + 1], zero)], axis=0
        )
        total = total + lax.dot_general(
            left, col_hot, (((1,), (1,)), ((), ())), preferred_element_type=f32
        )
    return total[:SPAN], total[SPAN:]


def deposited(field, change, strength):
    return jnp.concatenate(
        [field[:LOW], field[LOW:HIGH] + strength * change, field[HIGH:]], axis=0
    )


def place():
    t = lax.axis_index("trans")
    return lax.axis_index("beam"), t, t % 4, t // 4


def prep_body(phases, energy, row, col, weight, charge, send, own, charges):
    b, _, c, _ = place()
    one, two = jnp.where(c == 0, 2, 3), 3
    own_one, own_two = jnp.maximum(c - 2, 0), jnp.maximum(c - 1, 0)

    def pick(ref, index, target, slot):
        line = ref[pl.ds(index, 1), :].astype(f32)
        for q in range(ROWS):
            target[slot, q : q + 1, :] = line[:, q * WIDE : (q + 1) * WIDE]

    for slot, ref in enumerate((phases, energy, row, col, weight)):
        pick(ref, one, send, slot)
        pick(ref, own_one, own, slot)
    for slot, ref in enumerate((row, col, weight)):
        pick(ref, two, send, 5 + slot)
        pick(ref, own_two, own, 5 + slot)
    lane = lax.broadcasted_iota(jnp.int32, (8, 128), 1)
    line = jnp.zeros((8, 128), f32)
    for k in range(4):
        line = jnp.where(lane == 4 * b + k, charge[k].astype(f32) / charge_unit, line)
    for k in range(4):
        charges[k] = line


def pack_body(field, shifted, charges, out):
    line = jnp.sum(charges[...], axis=0)
    for c in range(4):
        for part in range(2):
            piece = shifted[part, c + 2] if c < 2 else field[part, c - 2]
            for half in range(2):
                at = (part * 2 + half) * 16
                for r in range(4):
                    out[4 * r + c, at : at + 16, :] = piece[:, half * 128 : (half + 1) * 128]
    for t in range(TRANS):
        out[t, 64:72, :] = line


def whole_field(x, part):
    halves = [
        x[:, (part * 2 + half) * 16 : (part * 2 + half + 1) * 16, :].reshape(GRID, 128)
        for half in range(2)
    ]
    return jnp.concatenate(halves, axis=1)


def chosen(own, received, slot, from_received):
    return jnp.where(from_received, received[slot], own[slot])


def first_body(x, own, received, rate, freq, amp, states, extra, re, im):
    b, _, c, _ = place()
    g = 4 * b + c
    take = lambda slot: chosen(own, received, slot, c < 2)
    fr, fi = whole_field(x, 0), whole_field(x, 1)
    probe(fr, fi, take(2), take(3), re, im)
    charges = jnp.max(x[:, 64:72, :], axis=0)
    source = lax.broadcasted_iota(jnp.int32, (8, 128), 1)
    pole = lax.broadcasted_iota(jnp.int32, (8, 128), 0)
    rates, freqs, amps = (jnp.zeros((8, 128), f32) for _ in range(3))
    for k in range(8):
        rates = jnp.where(pole == k, rate[k], rates)
        freqs = jnp.where(pole == k, freq[k], freqs)
        amps = jnp.where(pole == k, amp[k], amps)

    def total(value):
        return jnp.sum(jnp.sum(value, axis=0, keepdims=True), axis=1, keepdims=True)

    wakes, norms = [], []
    for back in (2, 1):
        s = (g + SLICES - back) % SLICES
        steps = jnp.maximum(s - source, 0).astype(f32)
        power = jnp.exp(-rates * steps) * jnp.cos(freqs * steps)
        reach = jnp.where(source < s, power, jnp.where(source == s, 0.5, 0.0))
        wakes.append(wake_gain / SLICES * total(amps * reach * charges))
        norms.append(total(jnp.where((source == s) & (pole == 0), charges, 0.0)))
    for k, value in enumerate((*wakes, *norms)):
        extra[k] = jnp.broadcast_to(value, (8, 128))
    angles = take(0)
    energies = (
        take(1) - kick_gain * (re[...] * jnp.cos(angles) - im[...] * jnp.sin(angles)) - wakes[0]
    )
    states[0] = angles + energies
    states[1] = energies


def second_body(x, states, own, received, extra, high, low, field, re, im):
    b, _, c, _ = place()
    take = lambda slot: chosen(own, received, slot, c < 2)
    br, bi = deposit(states[0], take(4), take(2), take(3))
    strength = deposit_gain * extra[2, 0:1, 0:1]
    fr = deposited(whole_field(x, 0), br, strength)
    fi = deposited(whole_field(x, 1), bi, strength)
    fr, fi = times_right(fr, fi, high, low)
    fr, fi = times_left(high[...].reshape(2 * GRID, GRID), low[...].reshape(2 * GRID, GRID), fr, fi)
    first = (b == 0) & (c == 1)
    fr = jnp.where(first, 0.0, fr)
    fi = jnp.where(first, 0.0, fi)
    field[0] = fr
    field[1] = fi
    take = lambda slot: chosen(own, received, slot, c < 1)
    probe(fr, fi, take(5), take(6), re, im)


def third_body(states, extra, re, im, out):
    angles = states[0]
    energies = (
        states[1]
        - kick_gain * (re[...] * jnp.cos(angles) - im[...] * jnp.sin(angles))
        - extra[1, 0:1, 0:1]
    )
    out[0] = angles + energies
    out[1] = energies


def fourth_body(field, states, own, received, extra, high, low, out):
    b, _, c, r = place()
    take = lambda slot: chosen(own, received, slot, c < 1)
    br, bi = deposit(states[0], take(7), take(5), take(6))
    strength = deposit_gain * extra[3, 0:1, 0:1]
    fr = deposited(field[0], br, strength)
    fi = deposited(field[1], bi, strength)
    at = pl.multiple_of(r * 64, 64)
    ah = jnp.concatenate([high[0, pl.ds(at, 64), :], high[1, pl.ds(at, 64), :]], axis=0)
    al = jnp.concatenate([low[0, pl.ds(at, 64), :], low[1, pl.ds(at, 64), :]], axis=0)
    fr, fi = times_left(ah, al, fr, fi)
    fr, fi = times_right(fr, fi, high, low)
    empty = (b == 0) & (c == 0)
    for part, value in enumerate((fr, fi)):
        value = jnp.where(empty, 0.0, value)
        for j in range(4):
            out[j, part * 16 : part * 16 + 16, :] = value[16 * j : 16 * j + 16]


def last_body(x, field, phase, energy):
    for c in range(4):
        for part in range(2):
            field[part, c] = x[c, part * 16 : part * 16 + 16, :]
        for k, target in enumerate((phase, energy)):
            for half in range(2):
                at = 32 + (k * 2 + half) * 8
                piece = x[c, at : at + 8, :]
                for q in range(ROWS):
                    begin = q * WIDE + half * 256
                    target[c : c + 1, begin : begin + 256] = piece[q : q + 1]


def call(body, outs, *args, scalars=(), plain=(), last=False):
    specs, inputs = [], []
    for k, arg in enumerate(args):
        specs.append(pl.BlockSpec(memory_space=pltpu.SMEM if k in scalars else pltpu.VMEM))
        if k not in scalars and k not in plain:
            arg = pltpu.with_memory_space_constraint(arg, pltpu.VMEM)
        inputs.append(arg)
    kind = jax.ShapeDtypeStruct if last else pltpu.VMEM
    return pl.pallas_call(
        body,
        out_shape=[kind(shape, f32) for shape in outs],
        in_specs=specs,
        out_specs=[pl.BlockSpec(memory_space=pltpu.VMEM) for _ in outs],
    )(*inputs)


def shards(
    field_in, phases, energy, row_cell, col_cell, weight, charge, pole_rate, pole_freq, pole_amp
):
    high, low = propagation_table()
    high, low = jnp.asarray(high), jnp.asarray(low)
    kept = (8, ROWS, WIDE)
    state_shape = (2, ROWS, WIDE)
    line = (ROWS, WIDE)
    shifted = lax.ppermute(field_in, "beam", NEXT_BEAM)
    send, own, charges = call(
        prep_body,
        [kept, kept, (4, 8, 128)],
        phases, energy, row_cell, col_cell, weight, charge,
        scalars=(5,), plain=range(5),
    )
    charges = lax.all_to_all(charges, JOINT, 0, 0, tiled=True, axis_index_groups=FOURS)
    received = lax.ppermute(send, JOINT, PAIR_TO_NEXT)
    (packed,) = call(pack_body, [(TRANS, 72, 128)], field_in, shifted, charges, plain=(0,))
    x = lax.all_to_all(packed, "trans", 0, 0, tiled=True)
    states, extra, _, _ = call(
        first_body,
        [state_shape, (4, 8, 128), line, line],
        x, own, received, pole_rate, pole_freq, pole_amp,
        scalars=(3, 4, 5),
    )
    following = lax.ppermute(states, JOINT, TO_PREVIOUS)
    field, re, im = call(
        second_body,
        [(2, GRID, GRID), line, line],
        x, states, own, received, extra, high, low, plain=(5, 6),
    )
    (final,) = call(third_body, [state_shape], following, extra, re, im)
    home = lax.ppermute(final, JOINT, TO_PREVIOUS)
    (bands,) = call(
        fourth_body, [(4, 32, GRID)], field, final, own, received, extra, high, low, plain=(5, 6)
    )
    home = jnp.concatenate([home[..., :256], home[..., 256:]], axis=1).reshape(32, 256)
    both = jnp.concatenate([bands, jnp.broadcast_to(home[None], (4, 32, 256))], axis=1)
    y = lax.all_to_all(both, "trans", 0, 0, tiled=True, axis_index_groups=QUADS)
    return tuple(
        call(last_body, [(2, 4, 16, GRID), (4, NPART), (4, NPART)], y, last=True)
    )


def solution(mesh):
    placed = (
        P(None, "beam", "trans", None),
        P("beam", None),
        P("beam", None),
        P("beam", None),
        P("beam", None),
        P("beam", None),
        P("beam"),
        P(),
        P(),
        P(),
    )
    return jax.shard_map(
        shards,
        mesh=mesh,
        in_specs=placed,
        out_specs=(P(None, "beam", "trans", None), P("beam", None), P("beam", None)),
        check_vma=False,
    )
```

```python
import functools
import math

import jax
import jax.numpy as jnp
import numpy as np
from jax import lax
from jax.experimental import pallas as pl
from jax.experimental.pallas import tpu as pltpu
from jax.sharding import PartitionSpec as P

diffraction = 20.0
kick_gain = 0.5
deposit_gain = 0.05
wake_gain = 3.0
charge_unit = 1024.0

GRID = 256
SLICES = 128
NPART = 4096
BEAM = 32
TRANS = 16
LOW, HIGH = 32, 224
SPAN = HIGH - LOW
ROWS, WIDE = 8, 512
JOINT = ("beam", "trans")
QUADS = [[4 * r + c for c in range(4)] for r in range(4)]

f32 = jnp.float32
bf16 = jnp.bfloat16


def propagation_table():
    n = np.arange(GRID)
    centred = ((n + GRID // 2) % GRID - GRID // 2) / GRID
    k = np.exp(-1j * diffraction * centred**2)
    h = np.fft.ifft(k)
    a = h[(n[:, None] - n[None, :]) % GRID]
    parts = np.stack([a.real, a.imag]).astype(np.float32)
    high = parts.astype(jnp.bfloat16)
    low = (parts - high.astype(np.float32)).astype(jnp.bfloat16)
    return high, low


def moved(fn):
    out = []
    for b in range(BEAM):
        for t in range(TRANS):
            b2, t2 = fn(b, t)
            out.append((b * TRANS + t, (b2 % BEAM) * TRANS + t2))
    return out


SPREAD = (
    (1, 4, 5), (3, 8, 11), (12, 20, 24), (7, 27, 28), (9, 16, 25), (2, 21, 23),
    (14, 19, 29), (15, 17, 30), (13, 18, 31), (6, 26, 28), (10, 22, 28),
)
FOURS = [
    [m * TRANS + t for m in group]
    for t in range(TRANS)
    for group in sorted({tuple(sorted([b, *(b ^ v for v in SPREAD[t % 11])])) for b in range(BEAM)})
]
TO_PREVIOUS = moved(lambda b, t: ((4 * b + t % 4 - 1) // 4, t // 4 * 4 + (t % 4 - 1) % 4))
NEXT_BEAM = [(b, (b + 1) % BEAM) for b in range(BEAM)]
PAIR_TO_NEXT = [
    (b * TRANS + t, (b + 1) % BEAM * TRANS + t)
    for b in range(BEAM)
    for t in range(TRANS)
    if t % 4 < 2
]


def split(x):
    high = x.astype(bf16)
    return high, (x - high.astype(f32)).astype(bf16)


def dot(a, b):
    return jnp.dot(a, b, preferred_element_type=f32)


def times_right(xr, xi, high, low):
    m = xr.shape[0]
    xh, xl = split(jnp.concatenate([xr, xi], axis=0))
    pr = dot(xh, high[0]) + dot(xl, high[0]) + dot(xh, low[0])
    pi = dot(xh, high[1]) + dot(xl, high[1]) + dot(xh, low[1])
    return pr[:m] - pi[m:], pi[:m] + pr[m:]


def times_left(ah, al, xr, xi):
    m = ah.shape[0] // 2
    rh, rl = split(xr)
    ih, il = split(xi)
    qr = dot(ah, rh) + dot(al, rh) + dot(ah, rl)
    qi = dot(ah, ih) + dot(al, ih) + dot(ah, il)
    return qr[:m] - qi[m:], qr[m:] + qi[:m]


def iota_rows(first, count):
    return lax.broadcasted_iota(jnp.int32, (count, WIDE), 0).astype(f32) + float(first)


def hot(values, rows_bf):
    return jnp.where(rows_bf == values.astype(bf16), jnp.ones((), bf16), jnp.zeros((), bf16))


def probe(fr, fi, rows, cols, out_re, out_im):
    high, low = split(jnp.concatenate([fr[LOW:HIGH], fi[LOW:HIGH]], axis=0))
    col_iota = iota_rows(0, GRID).astype(bf16)
    row_iota = iota_rows(LOW, SPAN)
    for q in range(ROWS):
        col_hot = hot(cols[q : q + 1], col_iota)
        found = dot(high, col_hot) + dot(low, col_hot)
        mask = row_iota == rows[q : q + 1]
        out_re[q : q + 1, :] = jnp.sum(jnp.where(mask, found[:SPAN], 0.0), axis=0, keepdims=True)
        out_im[q : q + 1, :] = jnp.sum(jnp.where(mask, found[SPAN:], 0.0), axis=0, keepdims=True)


def deposit(angles, weights, rows, cols):
    v = (weights * jnp.cos(angles)).astype(bf16)
    u = (-weights * jnp.sin(angles)).astype(bf16)
    col_iota = iota_rows(0, GRID).astype(bf16)
    row_iota = iota_rows(LOW, SPAN).astype(bf16)
    zero = jnp.zeros((), bf16)
    total = jnp.zeros((2 * SPAN, GRID), f32)
    for q in range(ROWS):
        col_hot = hot(cols[q : q + 1], col_iota)
        mask = row_iota == rows[q : q + 1].astype(bf16)
        left = jnp.concatenate(
            [jnp.where(mask, v[q : q + 1], zero), jnp.where(mask, u[q : q + 1], zero)], axis=0
        )
        total = total + lax.dot_general(
            left, col_hot, (((1,), (1,)), ((), ())), preferred_element_type=f32
        )
    return total[:SPAN], total[SPAN:]


def deposited(field, change, strength):
    return jnp.concatenate(
        [field[:LOW], field[LOW:HIGH] + strength * change, field[HIGH:]], axis=0
    )


def place():
    t = lax.axis_index("trans")
    return lax.axis_index("beam"), t, t % 4, t // 4


def prep_body(phases, energy, row, col, weight, charge, send, own, charges):
    b, _, c, _ = place()
    one, two = jnp.where(c == 0, 2, 3), 3
    own_one, own_two = jnp.maximum(c - 2, 0), jnp.maximum(c - 1, 0)

    def pick(ref, index, target, slot):
        line = ref[pl.ds(index, 1), :].astype(f32)
        for q in range(ROWS):
            target[slot, q : q + 1, :] = line[:, q * WIDE : (q + 1) * WIDE]

    for slot, ref in enumerate((phases, energy, row, col, weight)):
        pick(ref, one, send, slot)
        pick(ref, own_one, own, slot)
    for slot, ref in enumerate((row, col, weight)):
        pick(ref, two, send, 5 + slot)
        pick(ref, own_two, own, 5 + slot)
    lane = lax.broadcasted_iota(jnp.int32, (8, 128), 1)
    line = jnp.zeros((8, 128), f32)
    for k in range(4):
        line = jnp.where(lane == 4 * b + k, charge[k].astype(f32) / charge_unit, line)
    for k in range(4):
        charges[k] = line


def pack_body(field, shifted, charges, out):
    line = jnp.sum(charges[...], axis=0)
    for c in range(4):
        for part in range(2):
            piece = shifted[part, c + 2] if c < 2 else field[part, c - 2]
            for half in range(2):
                at = (part * 2 + half) * 16
                for r in range(4):
                    out[4 * r + c, at : at + 16, :] = piece[:, half * 128 : (half + 1) * 128]
    for t in range(TRANS):
        out[t, 64:72, :] = line


def whole_field(x, part):
    halves = [
        x[:, (part * 2 + half) * 16 : (part * 2 + half + 1) * 16, :].reshape(GRID, 128)
        for half in range(2)
    ]
    return jnp.concatenate(halves, axis=1)


def chosen(own, received, slot, from_received):
    return jnp.where(from_received, received[slot], own[slot])


def first_body(x, own, received, rate, freq, amp, states, extra, re, im):
    b, _, c, _ = place()
    g = 4 * b + c
    take = lambda slot: chosen(own, received, slot, c < 2)
    fr, fi = whole_field(x, 0), whole_field(x, 1)
    probe(fr, fi, take(2), take(3), re, im)
    charges = jnp.max(x[:, 64:72, :], axis=0)
    source = lax.broadcasted_iota(jnp.int32, (8, 128), 1)
    pole = lax.broadcasted_iota(jnp.int32, (8, 128), 0)
    rates, freqs, amps = (jnp.zeros((8, 128), f32) for _ in range(3))
    for k in range(8):
        rates = jnp.where(pole == k, rate[k], rates)
        freqs = jnp.where(pole == k, freq[k], freqs)
        amps = jnp.where(pole == k, amp[k], amps)

    def total(value):
        return jnp.sum(jnp.sum(value, axis=0, keepdims=True), axis=1, keepdims=True)

    wakes, norms = [], []
    for back in (2, 1):
        s = (g + SLICES - back) % SLICES
        steps = jnp.maximum(s - source, 0).astype(f32)
        power = jnp.exp(-rates * steps) * jnp.cos(freqs * steps)
        reach = jnp.where(source < s, power, jnp.where(source == s, 0.5, 0.0))
        wakes.append(wake_gain / SLICES * total(amps * reach * charges))
        norms.append(total(jnp.where((source == s) & (pole == 0), charges, 0.0)))
    for k, value in enumerate((*wakes, *norms)):
        extra[k] = jnp.broadcast_to(value, (8, 128))
    angles = take(0)
    energies = (
        take(1) - kick_gain * (re[...] * jnp.cos(angles) - im[...] * jnp.sin(angles)) - wakes[0]
    )
    states[0] = angles + energies
    states[1] = energies


def second_body(x, states, own, received, extra, high, low, field, re, im):
    b, _, c, _ = place()
    take = lambda slot: chosen(own, received, slot, c < 2)
    br, bi = deposit(states[0], take(4), take(2), take(3))
    strength = deposit_gain * extra[2, 0:1, 0:1]
    fr = deposited(whole_field(x, 0), br, strength)
    fi = deposited(whole_field(x, 1), bi, strength)
    fr, fi = times_right(fr, fi, high, low)
    fr, fi = times_left(high[...].reshape(2 * GRID, GRID), low[...].reshape(2 * GRID, GRID), fr, fi)
    first = (b == 0) & (c == 1)
    fr = jnp.where(first, 0.0, fr)
    fi = jnp.where(first, 0.0, fi)
    field[0] = fr
    field[1] = fi
    take = lambda slot: chosen(own, received, slot, c < 1)
    probe(fr, fi, take(5), take(6), re, im)


def third_body(states, extra, re, im, out):
    angles = states[0]
    energies = (
        states[1]
        - kick_gain * (re[...] * jnp.cos(angles) - im[...] * jnp.sin(angles))
        - extra[1, 0:1, 0:1]
    )
    out[0] = angles + energies
    out[1] = energies


def fourth_body(field, states, own, received, extra, high, low, out):
    b, _, c, r = place()
    take = lambda slot: chosen(own, received, slot, c < 1)
    br, bi = deposit(states[0], take(7), take(5), take(6))
    strength = deposit_gain * extra[3, 0:1, 0:1]
    fr = deposited(field[0], br, strength)
    fi = deposited(field[1], bi, strength)
    at = pl.multiple_of(r * 64, 64)
    ah = jnp.concatenate([high[0, pl.ds(at, 64), :], high[1, pl.ds(at, 64), :]], axis=0)
    al = jnp.concatenate([low[0, pl.ds(at, 64), :], low[1, pl.ds(at, 64), :]], axis=0)
    fr, fi = times_left(ah, al, fr, fi)
    fr, fi = times_right(fr, fi, high, low)
    empty = (b == 0) & (c == 0)
    for part, value in enumerate((fr, fi)):
        value = jnp.where(empty, 0.0, value)
        for j in range(4):
            out[j, part * 16 : part * 16 + 16, :] = value[16 * j : 16 * j + 16]


def last_body(x, field, phase, energy):
    for c in range(4):
        for part in range(2):
            field[part, c] = x[c, part * 16 : part * 16 + 16, :]
        for k, target in enumerate((phase, energy)):
            for half in range(2):
                at = 32 + (k * 2 + half) * 8
                piece = x[c, at : at + 8, :]
                for q in range(ROWS):
                    begin = q * WIDE + half * 256
                    target[c : c + 1, begin : begin + 256] = piece[q : q + 1]


def call(body, outs, *args, scalars=(), plain=(), last=False):
    specs, inputs = [], []
    for k, arg in enumerate(args):
        specs.append(pl.BlockSpec(memory_space=pltpu.SMEM if k in scalars else pltpu.VMEM))
        if k not in scalars and k not in plain:
            arg = pltpu.with_memory_space_constraint(arg, pltpu.VMEM)
        inputs.append(arg)
    kind = jax.ShapeDtypeStruct if last else pltpu.VMEM
    return pl.pallas_call(
        body,
        out_shape=[kind(shape, f32) for shape in outs],
        in_specs=specs,
        out_specs=[pl.BlockSpec(memory_space=pltpu.VMEM) for _ in outs],
    )(*inputs)


def shards(
    field_in, phases, energy, row_cell, col_cell, weight, charge, pole_rate, pole_freq, pole_amp
):
    high, low = propagation_table()
    high, low = jnp.asarray(high), jnp.asarray(low)
    kept = (8, ROWS, WIDE)
    state_shape = (2, ROWS, WIDE)
    line = (ROWS, WIDE)
    shifted = lax.ppermute(field_in, "beam", NEXT_BEAM)
    send, own, charges = call(
        prep_body,
        [kept, kept, (4, 8, 128)],
        phases, energy, row_cell, col_cell, weight, charge,
        scalars=(5,), plain=range(5),
    )
    charges = lax.all_to_all(charges, JOINT, 0, 0, tiled=True, axis_index_groups=FOURS)
    received = lax.ppermute(send, JOINT, PAIR_TO_NEXT)
    shifted, charges, received = lax.optimization_barrier((shifted, charges, received))
    (packed,) = call(pack_body, [(TRANS, 72, 128)], field_in, shifted, charges, plain=(0,))
    x = lax.all_to_all(packed, "trans", 0, 0, tiled=True)
    states, extra, _, _ = call(
        first_body,
        [state_shape, (4, 8, 128), line, line],
        x, own, received, pole_rate, pole_freq, pole_amp,
        scalars=(3, 4, 5),
    )
    following = lax.ppermute(states, JOINT, TO_PREVIOUS)
    field, re, im = call(
        second_body,
        [(2, GRID, GRID), line, line],
        x, states, own, received, extra, high, low, plain=(5, 6),
    )
    (final,) = call(third_body, [state_shape], following, extra, re, im)
    home = lax.ppermute(final, JOINT, TO_PREVIOUS)
    (bands,) = call(
        fourth_body, [(4, 32, GRID)], field, final, own, received, extra, high, low, plain=(5, 6)
    )
    home = jnp.concatenate([home[..., :256], home[..., 256:]], axis=1).reshape(32, 256)
    both = jnp.concatenate([bands, jnp.broadcast_to(home[None], (4, 32, 256))], axis=1)
    y = lax.all_to_all(both, "trans", 0, 0, tiled=True, axis_index_groups=QUADS)
    return tuple(
        call(last_body, [(2, 4, 16, GRID), (4, NPART), (4, NPART)], y, last=True)
    )


def solution(mesh):
    placed = (
        P(None, "beam", "trans", None),
        P("beam", None),
        P("beam", None),
        P("beam", None),
        P("beam", None),
        P("beam", None),
        P("beam"),
        P(),
        P(),
        P(),
    )
    return jax.shard_map(
        shards,
        mesh=mesh,
        in_specs=placed,
        out_specs=(P(None, "beam", "trans", None), P("beam", None), P("beam", None)),
        check_vma=False,
    )
```

```python
import functools

import jax
import jax.numpy as jnp
import numpy as np
from jax import lax
from jax.experimental import pallas as pl
from jax.experimental.pallas import tpu as pltpu
from jax.sharding import PartitionSpec as P

diffraction = 20.0
kick_gain = 0.5
deposit_gain = 0.05
wake_gain = 3.0
charge_unit = 1024.0

GRID = 256
SLICES = 128
NPART = 4096
BEAM = 32
TRANS = 16
LOW, HIGH = 32, 224
SPAN = HIGH - LOW
ROWS, WIDE = 8, 512
JOINT = ("beam", "trans")
QUADS = [[4 * r + c for c in range(4)] for r in range(4)]

f32 = jnp.float32
bf16 = jnp.bfloat16


def propagation_table():
    n = np.arange(GRID)
    centred = ((n + GRID // 2) % GRID - GRID // 2) / GRID
    k = np.exp(-1j * diffraction * centred**2)
    h = np.fft.ifft(k)
    a = h[(n[:, None] - n[None, :]) % GRID]
    parts = np.stack([a.real, a.imag]).astype(np.float32)
    high = parts.astype(jnp.bfloat16)
    low = (parts - high.astype(np.float32)).astype(jnp.bfloat16)
    return high, low


def moved(fn):
    out = []
    for b in range(BEAM):
        for t in range(TRANS):
            b2, t2 = fn(b, t)
            out.append((b * TRANS + t, (b2 % BEAM) * TRANS + t2))
    return out


TO_PREVIOUS = moved(lambda b, t: ((4 * b + t % 4 - 1) // 4, t // 4 * 4 + (t % 4 - 1) % 4))
NEXT_BEAM = [(b, (b + 1) % BEAM) for b in range(BEAM)]


def split(x):
    high = x.astype(bf16)
    return high, (x - high.astype(f32)).astype(bf16)


def dot(a, b):
    return jnp.dot(a, b, preferred_element_type=f32)


def times_right(xr, xi, high, low):
    m = xr.shape[0]
    xh, xl = split(jnp.concatenate([xr, xi], axis=0))
    pr = dot(xh, high[0]) + dot(xl, high[0]) + dot(xh, low[0])
    pi = dot(xh, high[1]) + dot(xl, high[1]) + dot(xh, low[1])
    return pr[:m] - pi[m:], pi[:m] + pr[m:]


def times_left(ah, al, xr, xi):
    m = ah.shape[0] // 2
    rh, rl = split(xr)
    ih, il = split(xi)
    qr = dot(ah, rh) + dot(al, rh) + dot(ah, rl)
    qi = dot(ah, ih) + dot(al, ih) + dot(ah, il)
    return qr[:m] - qi[m:], qr[m:] + qi[:m]


def iota_rows(first, count):
    return lax.broadcasted_iota(jnp.int32, (count, WIDE), 0).astype(f32) + float(first)


def hot(values, rows_bf):
    return jnp.where(rows_bf == values.astype(bf16), jnp.ones((), bf16), jnp.zeros((), bf16))


def probe(fr, fi, rows, cols, out_re, out_im):
    high, low = split(jnp.concatenate([fr[LOW:HIGH], fi[LOW:HIGH]], axis=0))
    col_iota = iota_rows(0, GRID).astype(bf16)
    row_iota = iota_rows(LOW, SPAN)
    for q in range(ROWS):
        col_hot = hot(cols[q : q + 1], col_iota)
        found = dot(high, col_hot) + dot(low, col_hot)
        mask = row_iota == rows[q : q + 1]
        out_re[q : q + 1, :] = jnp.sum(jnp.where(mask, found[:SPAN], 0.0), axis=0, keepdims=True)
        out_im[q : q + 1, :] = jnp.sum(jnp.where(mask, found[SPAN:], 0.0), axis=0, keepdims=True)


def deposit(angles, weights, rows, cols):
    v = (weights * jnp.cos(angles)).astype(bf16)
    u = (-weights * jnp.sin(angles)).astype(bf16)
    col_iota = iota_rows(0, GRID).astype(bf16)
    row_iota = iota_rows(LOW, SPAN).astype(bf16)
    zero = jnp.zeros((), bf16)
    total = [jnp.zeros((SPAN, GRID), f32)] * 2
    for q in range(ROWS):
        col_hot = hot(cols[q : q + 1], col_iota)
        mask = row_iota == rows[q : q + 1].astype(bf16)
        for k, value in enumerate((v, u)):
            left = jnp.where(mask, value[q : q + 1], zero)
            total[k] = total[k] + lax.dot_general(
                left, col_hot, (((1,), (1,)), ((), ())), preferred_element_type=f32
            )
    return total


def deposited(field, change, strength):
    return jnp.concatenate(
        [field[:LOW], field[LOW:HIGH] + strength * change, field[HIGH:]], axis=0
    )


def place():
    t = lax.axis_index("trans")
    return lax.axis_index("beam"), t, t % 4, t // 4


def prep_body(field, phases, energy, row, col, weight, send, own):
    _, _, c, _ = place()
    for part in range(2):
        for k in range(2):
            send[part * 2 + k] = field[part, 2 + k]
    own_one, own_two = jnp.maximum(c - 2, 0), jnp.maximum(c - 1, 0)

    def pick(ref, index, slot):
        line = ref[pl.ds(index, 1), :].astype(f32)
        for q in range(ROWS):
            own[slot, q : q + 1, :] = line[:, q * WIDE : (q + 1) * WIDE]

    for slot, ref in enumerate((phases, energy, row, col, weight)):
        pick(ref, own_one, slot)
        for k in range(2):
            line = ref[2 + k : 3 + k, :].astype(f32)
            for q in range(ROWS):
                for half in range(2):
                    begin = q * WIDE + half * 256
                    at = half * 8 + q
                    send[4 + 2 * slot + k, at : at + 1, :] = line[:, begin : begin + 256]
    for slot, ref in enumerate((row, col, weight)):
        pick(ref, own_two, 5 + slot)


def line_body(charge, charges):
    b, _, _, _ = place()
    lane = lax.broadcasted_iota(jnp.int32, (8, 128), 1)
    line = jnp.zeros((8, 128), f32)
    for k in range(4):
        line = jnp.where(lane == 4 * b + k, charge[k].astype(f32) / charge_unit, line)
    for k in range(BEAM):
        charges[k] = line


def pack_body(field, received, out):
    for c in range(4):
        for part in range(2):
            piece = received[part * 2 + c] if c < 2 else field[part, c - 2]
            for half in range(2):
                at = (part * 2 + half) * 16
                for r in range(4):
                    out[4 * r + c, at : at + 16, :] = piece[:, half * 128 : (half + 1) * 128]


def whole_field(x, part):
    halves = [
        x[:, (part * 2 + half) * 16 : (part * 2 + half + 1) * 16, :].reshape(GRID, 128)
        for half in range(2)
    ]
    return jnp.concatenate(halves, axis=1)


def period_one(own, received, c, slot):
    piece = received[4 + 2 * slot + jnp.minimum(c, 1)]
    piece = jnp.concatenate([piece[:8], piece[8:]], axis=1)
    return jnp.where(c < 2, piece, own[slot])


def period_two(own, received, c, slot):
    piece = received[4 + 2 * slot + 1]
    piece = jnp.concatenate([piece[:8], piece[8:]], axis=1)
    return jnp.where(c < 1, piece, own[slot + 3])


def wake_body(gathered, rate, freq, amp, extra):
    b, _, c, _ = place()
    g = 4 * b + c
    charges = jnp.sum(gathered[...], axis=0)
    source = lax.broadcasted_iota(jnp.int32, (8, 128), 1)
    pole = lax.broadcasted_iota(jnp.int32, (8, 128), 0)
    rates, freqs, amps = (jnp.zeros((8, 128), f32) for _ in range(3))
    for k in range(8):
        rates = jnp.where(pole == k, rate[k], rates)
        freqs = jnp.where(pole == k, freq[k], freqs)
        amps = jnp.where(pole == k, amp[k], amps)

    def total(value):
        return jnp.sum(jnp.sum(value, axis=0, keepdims=True), axis=1, keepdims=True)

    for k, back in enumerate((2, 1)):
        s = (g + SLICES - back) % SLICES
        steps = jnp.maximum(s - source, 0).astype(f32)
        power = jnp.exp(-rates * steps) * jnp.cos(freqs * steps)
        reach = jnp.where(source < s, power, jnp.where(source == s, 0.5, 0.0))
        wake = wake_gain / SLICES * total(amps * reach * charges)
        norm = total(jnp.where((source == s) & (pole == 0), charges, 0.0))
        extra[k] = jnp.broadcast_to(wake, (8, 128))
        extra[2 + k] = jnp.broadcast_to(norm, (8, 128))


def first_body(x, own, received, extra, states, re, im):
    _, _, c, _ = place()
    take = functools.partial(period_one, own, received, c)
    fr, fi = whole_field(x, 0), whole_field(x, 1)
    probe(fr, fi, take(2), take(3), re, im)
    angles = take(0)
    energies = (
        take(1)
        - kick_gain * (re[...] * jnp.cos(angles) - im[...] * jnp.sin(angles))
        - extra[0, 0:1, 0:1]
    )
    states[0] = angles + energies
    states[1] = energies


def second_body(x, states, own, received, extra, high, low, field, re, im):
    b, _, c, _ = place()
    take = functools.partial(period_one, own, received, c)
    br, bi = deposit(states[0], take(4), take(2), take(3))
    strength = deposit_gain * extra[2, 0:1, 0:1]
    fr = deposited(whole_field(x, 0), br, strength)
    fi = deposited(whole_field(x, 1), bi, strength)
    fr, fi = times_right(fr, fi, high, low)
    fr, fi = times_left(high[...].reshape(2 * GRID, GRID), low[...].reshape(2 * GRID, GRID), fr, fi)
    first = (b == 0) & (c == 1)
    fr = jnp.where(first, 0.0, fr)
    fi = jnp.where(first, 0.0, fi)
    field[0] = fr
    field[1] = fi
    take = functools.partial(period_two, own, received, c)
    probe(fr, fi, take(2), take(3), re, im)


def third_body(states, extra, re, im, out):
    angles = states[0]
    energies = (
        states[1]
        - kick_gain * (re[...] * jnp.cos(angles) - im[...] * jnp.sin(angles))
        - extra[1, 0:1, 0:1]
    )
    out[0] = angles + energies
    out[1] = energies


def fourth_body(field, states, own, received, extra, high, low, out):
    b, _, c, r = place()
    take = functools.partial(period_two, own, received, c)
    br, bi = deposit(states[0], take(4), take(2), take(3))
    strength = deposit_gain * extra[3, 0:1, 0:1]
    fr = deposited(field[0], br, strength)
    fi = deposited(field[1], bi, strength)
    at = pl.multiple_of(r * 64, 64)
    ah = jnp.concatenate([high[0, pl.ds(at, 64), :], high[1, pl.ds(at, 64), :]], axis=0)
    al = jnp.concatenate([low[0, pl.ds(at, 64), :], low[1, pl.ds(at, 64), :]], axis=0)
    fr, fi = times_left(ah, al, fr, fi)
    fr, fi = times_right(fr, fi, high, low)
    empty = (b == 0) & (c == 0)
    for part, value in enumerate((fr, fi)):
        value = jnp.where(empty, 0.0, value)
        for j in range(4):
            out[j, part * 16 : part * 16 + 16, :] = value[16 * j : 16 * j + 16]


def last_body(x, field, phase, energy):
    for c in range(4):
        for part in range(2):
            field[part, c] = x[c, part * 16 : part * 16 + 16, :]
        for k, target in enumerate((phase, energy)):
            for half in range(2):
                at = 32 + (k * 2 + half) * 8
                piece = x[c, at : at + 8, :]
                for q in range(ROWS):
                    begin = q * WIDE + half * 256
                    target[c : c + 1, begin : begin + 256] = piece[q : q + 1]


def call(body, outs, *args, scalars=(), plain=(), last=False):
    specs, inputs = [], []
    for k, arg in enumerate(args):
        specs.append(pl.BlockSpec(memory_space=pltpu.SMEM if k in scalars else pltpu.VMEM))
        if k not in scalars and k not in plain:
            arg = pltpu.with_memory_space_constraint(arg, pltpu.VMEM)
        inputs.append(arg)
    kind = jax.ShapeDtypeStruct if last else pltpu.VMEM
    return pl.pallas_call(
        body,
        out_shape=[kind(shape, f32) for shape in outs],
        in_specs=specs,
        out_specs=[pl.BlockSpec(memory_space=pltpu.VMEM) for _ in outs],
    )(*inputs)


def shards(
    field_in, phases, energy, row_cell, col_cell, weight, charge, pole_rate, pole_freq, pole_amp
):
    high, low = propagation_table()
    high, low = jnp.asarray(high), jnp.asarray(low)
    kept = (8, ROWS, WIDE)
    state_shape = (2, ROWS, WIDE)
    line = (ROWS, WIDE)
    send, own = call(
        prep_body,
        [(14, 16, GRID), kept],
        field_in, phases, energy, row_cell, col_cell, weight,
        plain=range(6),
    )
    received = lax.ppermute(send, "beam", NEXT_BEAM)
    (charges,) = call(line_body, [(BEAM, 8, 128)], charge, scalars=(0,))
    charges = lax.all_to_all(charges, "beam", 0, 0, tiled=True)
    (extra,) = call(
        wake_body, [(4, 8, 128)], charges, pole_rate, pole_freq, pole_amp, scalars=(1, 2, 3)
    )
    (packed,) = call(pack_body, [(TRANS, 64, 128)], field_in, received, plain=(0,))
    x = lax.all_to_all(packed, "trans", 0, 0, tiled=True)
    states, _, _ = call(
        first_body, [state_shape, line, line], x, own, received, extra
    )
    following = lax.ppermute(states, JOINT, TO_PREVIOUS)
    field, re, im = call(
        second_body,
        [(2, GRID, GRID), line, line],
        x, states, own, received, extra, high, low, plain=(5, 6),
    )
    (final,) = call(third_body, [state_shape], following, extra, re, im)
    home = lax.ppermute(final, JOINT, TO_PREVIOUS)
    (bands,) = call(
        fourth_body, [(4, 32, GRID)], field, final, own, received, extra, high, low, plain=(5, 6)
    )
    home = jnp.concatenate([home[..., :256], home[..., 256:]], axis=1).reshape(32, 256)
    both = jnp.concatenate([bands, jnp.broadcast_to(home[None], (4, 32, 256))], axis=1)
    y = lax.all_to_all(both, "trans", 0, 0, tiled=True, axis_index_groups=QUADS)
    return tuple(
        call(last_body, [(2, 4, 16, GRID), (4, NPART), (4, NPART)], y, last=True)
    )


def solution(mesh):
    placed = (
        P(None, "beam", "trans", None),
        P("beam", None),
        P("beam", None),
        P("beam", None),
        P("beam", None),
        P("beam", None),
        P("beam"),
        P(),
        P(),
        P(),
    )
    return jax.shard_map(
        shards,
        mesh=mesh,
        in_specs=placed,
        out_specs=(P(None, "beam", "trans", None), P("beam", None), P("beam", None)),
        check_vma=False,
    )
```

```python
import functools

import jax
import jax.numpy as jnp
import numpy as np
from jax import lax
from jax.experimental import pallas as pl
from jax.experimental.pallas import tpu as pltpu
from jax.sharding import PartitionSpec as P

diffraction = 20.0
kick_gain = 0.5
deposit_gain = 0.05
wake_gain = 3.0
charge_unit = 1024.0

GRID = 256
SLICES = 128
NPART = 4096
BEAM = 32
TRANS = 16
LOW, HIGH = 32, 224
SPAN = HIGH - LOW
ROWS, WIDE = 8, 512
JOINT = ("beam", "trans")
QUADS = [[4 * r + c for c in range(4)] for r in range(4)]

f32 = jnp.float32
bf16 = jnp.bfloat16


def propagation_table():
    n = np.arange(GRID)
    centred = ((n + GRID // 2) % GRID - GRID // 2) / GRID
    k = np.exp(-1j * diffraction * centred**2)
    h = np.fft.ifft(k)
    a = h[(n[:, None] - n[None, :]) % GRID]
    parts = np.stack([a.real, a.imag]).astype(np.float32)
    high = parts.astype(jnp.bfloat16)
    low = (parts - high.astype(np.float32)).astype(jnp.bfloat16)
    tall = np.stack([part.reshape(2 * GRID, GRID) for part in (high, low)])
    wide = np.stack([np.concatenate([part[0], part[1]], axis=1) for part in (high, low)])
    return wide, tall


def moved(fn):
    out = []
    for b in range(BEAM):
        for t in range(TRANS):
            b2, t2 = fn(b, t)
            out.append((b * TRANS + t, (b2 % BEAM) * TRANS + t2))
    return out


TO_PREVIOUS = moved(lambda b, t: ((4 * b + t % 4 - 1) // 4, t // 4 * 4 + (t % 4 - 1) % 4))
NEXT_BEAM = [(b, (b + 1) % BEAM) for b in range(BEAM)]


def split(x):
    high = x.astype(bf16)
    return high, (x - high.astype(f32)).astype(bf16)


def dot(a, b):
    return jnp.dot(a, b, preferred_element_type=f32)


def times_right(xr, xi, high, low):
    p = []
    for x in (xr, xi):
        xh, xl = split(x)
        p.append(dot(xh, high) + dot(xl, high) + dot(xh, low))
    return p[0][:, :GRID] - p[1][:, GRID:], p[0][:, GRID:] + p[1][:, :GRID]


def times_left(ah, al, xr, xi):
    m = ah.shape[0] // 2
    xh, xl = split(jnp.concatenate([xr, xi], axis=1))
    q = []
    for k in range(2):
        high, low = ah[k * m : (k + 1) * m], al[k * m : (k + 1) * m]
        q.append(dot(high, xh) + dot(low, xh) + dot(high, xl))
    return q[0][:, :GRID] - q[1][:, GRID:], q[1][:, :GRID] + q[0][:, GRID:]


def iota_rows(first, count):
    return lax.broadcasted_iota(jnp.int32, (count, WIDE), 0).astype(f32) + float(first)


def hot(values, rows_bf):
    return jnp.where(rows_bf == values.astype(bf16), jnp.ones((), bf16), jnp.zeros((), bf16))


def probe(fr, fi, rows, cols, out_re, out_im):
    high, low = split(jnp.concatenate([fr[LOW:HIGH], fi[LOW:HIGH]], axis=0))
    col_iota = iota_rows(0, GRID).astype(bf16)
    row_iota = iota_rows(LOW, SPAN)
    for q in range(ROWS):
        col_hot = hot(cols[q : q + 1], col_iota)
        found = dot(high, col_hot) + dot(low, col_hot)
        mask = row_iota == rows[q : q + 1]
        out_re[q : q + 1, :] = jnp.sum(jnp.where(mask, found[:SPAN], 0.0), axis=0, keepdims=True)
        out_im[q : q + 1, :] = jnp.sum(jnp.where(mask, found[SPAN:], 0.0), axis=0, keepdims=True)


def deposit(angles, weights, rows, cols):
    v = (weights * jnp.cos(angles)).astype(bf16)
    u = (-weights * jnp.sin(angles)).astype(bf16)
    col_iota = iota_rows(0, GRID).astype(bf16)
    row_iota = iota_rows(LOW, SPAN).astype(bf16)
    zero = jnp.zeros((), bf16)
    total = [jnp.zeros((SPAN, GRID), f32)] * 2
    for q in range(ROWS):
        col_hot = hot(cols[q : q + 1], col_iota)
        mask = row_iota == rows[q : q + 1].astype(bf16)
        for k, value in enumerate((v, u)):
            left = jnp.where(mask, value[q : q + 1], zero)
            total[k] = total[k] + lax.dot_general(
                left, col_hot, (((1,), (1,)), ((), ())), preferred_element_type=f32
            )
    return total


def deposited(field, change, strength):
    return jnp.concatenate(
        [field[:LOW], field[LOW:HIGH] + strength * change, field[HIGH:]], axis=0
    )


def place():
    t = lax.axis_index("trans")
    return lax.axis_index("beam"), t, t % 4, t // 4


def prep_body(field, phases, energy, row, col, weight, charge, send, own, charges):
    b, _, c, _ = place()
    for part in range(2):
        for k in range(2):
            send[part * 2 + k] = field[part, 2 + k]
    own_one, own_two = jnp.maximum(c - 2, 0), jnp.maximum(c - 1, 0)

    def pick(ref, index, slot):
        line = ref[pl.ds(index, 1), :].astype(f32)
        for q in range(ROWS):
            own[slot, q : q + 1, :] = line[:, q * WIDE : (q + 1) * WIDE]

    for slot, ref in enumerate((phases, energy, row, col, weight)):
        pick(ref, own_one, slot)
        for k in range(2):
            line = ref[2 + k : 3 + k, :].astype(f32)
            for q in range(ROWS):
                for half in range(2):
                    begin = q * WIDE + half * 256
                    at = half * 8 + q
                    send[4 + 2 * slot + k, at : at + 1, :] = line[:, begin : begin + 256]
    for slot, ref in enumerate((row, col, weight)):
        pick(ref, own_two, 5 + slot)
    lane = lax.broadcasted_iota(jnp.int32, (1, SLICES), 1)
    line = jnp.zeros((1, SLICES), f32)
    for k in range(4):
        line = jnp.where(lane == 4 * b + k, charge[k].astype(f32) / charge_unit, line)
    charges[...] = line


def pack_body(field, received, out):
    for c in range(4):
        for part in range(2):
            piece = received[part * 2 + c] if c < 2 else field[part, c - 2]
            for half in range(2):
                at = (part * 2 + half) * 16
                for r in range(4):
                    out[4 * r + c, at : at + 16, :] = piece[:, half * 128 : (half + 1) * 128]


def whole_field(x, part):
    halves = [
        x[:, (part * 2 + half) * 16 : (part * 2 + half + 1) * 16, :].reshape(GRID, 128)
        for half in range(2)
    ]
    return jnp.concatenate(halves, axis=1)


def period_one(own, received, c, slot):
    piece = received[4 + 2 * slot + jnp.minimum(c, 1)]
    piece = jnp.concatenate([piece[:8], piece[8:]], axis=1)
    return jnp.where(c < 2, piece, own[slot])


def period_two(own, received, c, slot):
    piece = received[4 + 2 * slot + 1]
    piece = jnp.concatenate([piece[:8], piece[8:]], axis=1)
    return jnp.where(c < 1, piece, own[slot + 3])


def wake_sums(g, charges, rate, freq, amp, extra):
    source = lax.broadcasted_iota(jnp.int32, (8, 128), 1)
    pole = lax.broadcasted_iota(jnp.int32, (8, 128), 0)
    rates, freqs, amps = (jnp.zeros((8, 128), f32) for _ in range(3))
    for k in range(8):
        rates = jnp.where(pole == k, rate[k], rates)
        freqs = jnp.where(pole == k, freq[k], freqs)
        amps = jnp.where(pole == k, amp[k], amps)

    def total(value):
        return jnp.sum(jnp.sum(value, axis=0, keepdims=True), axis=1, keepdims=True)

    for k, back in enumerate((2, 1)):
        s = (g + SLICES - back) % SLICES
        steps = jnp.maximum(s - source, 0).astype(f32)
        power = jnp.exp(-rates * steps) * jnp.cos(freqs * steps)
        reach = jnp.where(source < s, power, jnp.where(source == s, 0.5, 0.0))
        wake = wake_gain / SLICES * total(amps * reach * charges)
        norm = total(jnp.where((source == s) & (pole == 0), charges, 0.0))
        extra[k] = jnp.broadcast_to(wake, (8, 128))
        extra[2 + k] = jnp.broadcast_to(norm, (8, 128))


def first_body(x, own, received, charges, rate, freq, amp, states, extra, re, im):
    b, _, c, _ = place()
    wake_sums(4 * b + c, charges[...], rate, freq, amp, extra)
    take = functools.partial(period_one, own, received, c)
    fr, fi = whole_field(x, 0), whole_field(x, 1)
    probe(fr, fi, take(2), take(3), re, im)
    angles = take(0)
    energies = (
        take(1)
        - kick_gain * (re[...] * jnp.cos(angles) - im[...] * jnp.sin(angles))
        - extra[0, 0:1, 0:1]
    )
    states[0] = angles + energies
    states[1] = energies


def second_body(x, states, own, received, extra, wide, tall, field, re, im):
    b, _, c, _ = place()
    take = functools.partial(period_one, own, received, c)
    br, bi = deposit(states[0], take(4), take(2), take(3))
    strength = deposit_gain * extra[2, 0:1, 0:1]
    fr = deposited(whole_field(x, 0), br, strength)
    fi = deposited(whole_field(x, 1), bi, strength)
    fr, fi = times_right(fr, fi, wide[0], wide[1])
    fr, fi = times_left(tall[0], tall[1], fr, fi)
    first = (b == 0) & (c == 1)
    fr = jnp.where(first, 0.0, fr)
    fi = jnp.where(first, 0.0, fi)
    field[0] = fr
    field[1] = fi
    take = functools.partial(period_two, own, received, c)
    probe(fr, fi, take(2), take(3), re, im)


def third_body(states, extra, re, im, out):
    angles = states[0]
    energies = (
        states[1]
        - kick_gain * (re[...] * jnp.cos(angles) - im[...] * jnp.sin(angles))
        - extra[1, 0:1, 0:1]
    )
    out[0] = angles + energies
    out[1] = energies


def fourth_body(field, states, own, received, extra, wide, tall, out):
    b, _, c, r = place()
    take = functools.partial(period_two, own, received, c)
    br, bi = deposit(states[0], take(4), take(2), take(3))
    strength = deposit_gain * extra[3, 0:1, 0:1]
    fr = deposited(field[0], br, strength)
    fi = deposited(field[1], bi, strength)
    at = pl.multiple_of(r * 64, 64)
    ah, al = (
        jnp.concatenate([tall[k, pl.ds(at, 64), :], tall[k, pl.ds(GRID + at, 64), :]], axis=0)
        for k in range(2)
    )
    fr, fi = times_left(ah, al, fr, fi)
    fr, fi = times_right(fr, fi, wide[0], wide[1])
    empty = (b == 0) & (c == 0)
    for part, value in enumerate((fr, fi)):
        value = jnp.where(empty, 0.0, value)
        for j in range(4):
            out[j, part * 16 : part * 16 + 16, :] = value[16 * j : 16 * j + 16]


def last_body(x, field, phase, energy):
    for c in range(4):
        for part in range(2):
            field[part, c] = x[c, part * 16 : part * 16 + 16, :]
        for k, target in enumerate((phase, energy)):
            for half in range(2):
                at = 32 + (k * 2 + half) * 8
                piece = x[c, at : at + 8, :]
                for q in range(ROWS):
                    begin = q * WIDE + half * 256
                    target[c : c + 1, begin : begin + 256] = piece[q : q + 1]


def call(body, outs, *args, scalars=(), plain=(), last=False):
    specs, inputs = [], []
    for k, arg in enumerate(args):
        specs.append(pl.BlockSpec(memory_space=pltpu.SMEM if k in scalars else pltpu.VMEM))
        if k not in scalars and k not in plain:
            arg = pltpu.with_memory_space_constraint(arg, pltpu.VMEM)
        inputs.append(arg)
    kind = jax.ShapeDtypeStruct if last else pltpu.VMEM
    return pl.pallas_call(
        body,
        out_shape=[kind(shape, f32) for shape in outs],
        in_specs=specs,
        out_specs=[pl.BlockSpec(memory_space=pltpu.VMEM) for _ in outs],
    )(*inputs)


def shards(
    field_in, phases, energy, row_cell, col_cell, weight, charge, pole_rate, pole_freq, pole_amp
):
    wide, tall = (jnp.asarray(table) for table in propagation_table())
    kept = (8, ROWS, WIDE)
    state_shape = (2, ROWS, WIDE)
    line = (ROWS, WIDE)
    send, own, charges = call(
        prep_body,
        [(14, 16, GRID), kept, (1, SLICES)],
        field_in, phases, energy, row_cell, col_cell, weight, charge,
        scalars=(6,), plain=range(6),
    )
    received = lax.ppermute(send, "beam", NEXT_BEAM)
    charges = jnp.broadcast_to(charges[None], (BEAM, 1, SLICES))
    charges = lax.all_to_all(charges, "beam", 0, 0, tiled=True)
    charges = jnp.sum(charges, axis=0)
    (packed,) = call(pack_body, [(TRANS, 64, 128)], field_in, received, plain=(0,))
    x = lax.all_to_all(packed, "trans", 0, 0, tiled=True)
    states, extra, _, _ = call(
        first_body,
        [state_shape, (4, 8, 128), line, line],
        x, own, received, charges, pole_rate, pole_freq, pole_amp,
        scalars=(4, 5, 6),
    )
    following = lax.ppermute(states, JOINT, TO_PREVIOUS)
    field, re, im = call(
        second_body,
        [(2, GRID, GRID), line, line],
        x, states, own, received, extra, wide, tall, plain=(5, 6),
    )
    (final,) = call(third_body, [state_shape], following, extra, re, im)
    home = lax.ppermute(final, JOINT, TO_PREVIOUS)
    (bands,) = call(
        fourth_body, [(4, 32, GRID)], field, final, own, received, extra, wide, tall, plain=(5, 6)
    )
    home = jnp.concatenate([home[..., :256], home[..., 256:]], axis=1).reshape(32, 256)
    both = jnp.concatenate([bands, jnp.broadcast_to(home[None], (4, 32, 256))], axis=1)
    y = lax.all_to_all(both, "trans", 0, 0, tiled=True, axis_index_groups=QUADS)
    return tuple(
        call(last_body, [(2, 4, 16, GRID), (4, NPART), (4, NPART)], y, last=True)
    )


def solution(mesh):
    placed = (
        P(None, "beam", "trans", None),
        P("beam", None),
        P("beam", None),
        P("beam", None),
        P("beam", None),
        P("beam", None),
        P("beam"),
        P(),
        P(),
        P(),
    )
    return jax.shard_map(
        shards,
        mesh=mesh,
        in_specs=placed,
        out_specs=(P(None, "beam", "trans", None), P("beam", None), P("beam", None)),
        check_vma=False,
    )
```

```python
import functools

import jax
import jax.numpy as jnp
import numpy as np
from jax import lax
from jax.experimental import pallas as pl
from jax.experimental.pallas import tpu as pltpu
from jax.sharding import PartitionSpec as P

diffraction = 20.0
kick_gain = 0.5
deposit_gain = 0.05
wake_gain = 3.0
charge_unit = 1024.0

GRID = 256
SLICES = 128
NPART = 4096
BEAM = 32
TRANS = 16
LOW, HIGH = 32, 224
SPAN = HIGH - LOW
TABLE = (2, 2 * GRID, GRID)
ROWS, WIDE = 8, 512
JOINT = ("beam", "trans")
QUADS = [[4 * r + c for c in range(4)] for r in range(4)]

f32 = jnp.float32
bf16 = jnp.bfloat16


def propagation_table():
    n = np.arange(GRID)
    centred = ((n + GRID // 2) % GRID - GRID // 2) / GRID
    k = np.exp(-1j * diffraction * centred**2)
    h = np.fft.ifft(k)
    a = h[(n[:, None] - n[None, :]) % GRID]
    parts = np.stack([a.real, a.imag]).astype(np.float32)
    high = parts.astype(jnp.bfloat16)
    low = (parts - high.astype(np.float32)).astype(jnp.bfloat16)
    return np.stack([part.reshape(2 * GRID, GRID) for part in (high, low)])


def moved(fn):
    out = []
    for b in range(BEAM):
        for t in range(TRANS):
            b2, t2 = fn(b, t)
            out.append((b * TRANS + t, (b2 % BEAM) * TRANS + t2))
    return out


TO_PREVIOUS = moved(lambda b, t: ((4 * b + t % 4 - 1) // 4, t // 4 * 4 + (t % 4 - 1) % 4))
NEXT_BEAM = [(b, (b + 1) % BEAM) for b in range(BEAM)]


def split(x):
    high = x.astype(bf16)
    return high, (x - high.astype(f32)).astype(bf16)


def dot(a, b):
    return jnp.dot(a, b, preferred_element_type=f32)


def times_right(xr, xi, high, low):
    p = []
    for x in (xr, xi):
        xh, xl = split(x)
        for k in range(2):
            h, w = high[k * GRID : (k + 1) * GRID], low[k * GRID : (k + 1) * GRID]
            p.append(dot(xh, h) + dot(xl, h) + dot(xh, w))
    return p[0] - p[3], p[1] + p[2]


def times_left(ah, al, xr, xi):
    m = ah.shape[0] // 2
    xh, xl = split(jnp.concatenate([xr, xi], axis=1))
    q = []
    for k in range(2):
        high, low = ah[k * m : (k + 1) * m], al[k * m : (k + 1) * m]
        q.append(dot(high, xh) + dot(low, xh) + dot(high, xl))
    return q[0][:, :GRID] - q[1][:, GRID:], q[1][:, :GRID] + q[0][:, GRID:]


def iota_rows(first, count):
    return lax.broadcasted_iota(jnp.int32, (count, WIDE), 0).astype(f32) + float(first)


def hot(values, rows_bf):
    return jnp.where(rows_bf == values.astype(bf16), jnp.ones((), bf16), jnp.zeros((), bf16))


def probe(fr, fi, rows, cols, out_re, out_im):
    high, low = split(jnp.concatenate([fr[LOW:HIGH], fi[LOW:HIGH]], axis=0))
    col_iota = iota_rows(0, GRID).astype(bf16)
    row_iota = iota_rows(LOW, SPAN)
    for q in range(ROWS):
        col_hot = hot(cols[q : q + 1], col_iota)
        found = dot(high, col_hot) + dot(low, col_hot)
        mask = row_iota == rows[q : q + 1]
        out_re[q : q + 1, :] = jnp.sum(jnp.where(mask, found[:SPAN], 0.0), axis=0, keepdims=True)
        out_im[q : q + 1, :] = jnp.sum(jnp.where(mask, found[SPAN:], 0.0), axis=0, keepdims=True)


def deposit(angles, weights, rows, cols):
    v = (weights * jnp.cos(angles)).astype(bf16)
    u = (-weights * jnp.sin(angles)).astype(bf16)
    col_iota = iota_rows(0, GRID).astype(bf16)
    row_iota = iota_rows(LOW, SPAN).astype(bf16)
    zero = jnp.zeros((), bf16)
    total = [jnp.zeros((SPAN, GRID), f32)] * 2
    for q in range(ROWS):
        col_hot = hot(cols[q : q + 1], col_iota)
        mask = row_iota == rows[q : q + 1].astype(bf16)
        for k, value in enumerate((v, u)):
            left = jnp.where(mask, value[q : q + 1], zero)
            total[k] = total[k] + lax.dot_general(
                left, col_hot, (((1,), (1,)), ((), ())), preferred_element_type=f32
            )
    return total


def deposited(field, change, strength):
    return jnp.concatenate(
        [field[:LOW], field[LOW:HIGH] + strength * change, field[HIGH:]], axis=0
    )


def place():
    t = lax.axis_index("trans")
    return lax.axis_index("beam"), t, t % 4, t // 4


def prep_body(field, phases, energy, row, col, weight, charge, send, own, charges):
    b, _, c, _ = place()
    for part in range(2):
        for k in range(2):
            send[part * 2 + k] = field[part, 2 + k]
    own_one, own_two = jnp.maximum(c - 2, 0), jnp.maximum(c - 1, 0)

    def pick(ref, index, slot):
        line = ref[pl.ds(index, 1), :].astype(f32)
        for q in range(ROWS):
            own[slot, q : q + 1, :] = line[:, q * WIDE : (q + 1) * WIDE]

    for slot, ref in enumerate((phases, energy, row, col, weight)):
        pick(ref, own_one, slot)
        for k in range(2):
            line = ref[2 + k : 3 + k, :].astype(f32)
            for q in range(ROWS):
                for half in range(2):
                    begin = q * WIDE + half * 256
                    at = half * 8 + q
                    send[4 + 2 * slot + k, at : at + 1, :] = line[:, begin : begin + 256]
    for slot, ref in enumerate((row, col, weight)):
        pick(ref, own_two, 5 + slot)
    lane = lax.broadcasted_iota(jnp.int32, (1, SLICES), 1)
    line = jnp.zeros((1, SLICES), f32)
    for k in range(4):
        line = jnp.where(lane == 4 * b + k, charge[k].astype(f32) / charge_unit, line)
    charges[...] = line


def pack_body(field, received, out):
    for c in range(4):
        for part in range(2):
            piece = received[part * 2 + c] if c < 2 else field[part, c - 2]
            for half in range(2):
                at = (part * 2 + half) * 16
                for r in range(4):
                    out[4 * r + c, at : at + 16, :] = piece[:, half * 128 : (half + 1) * 128]


def whole_field(x, part):
    halves = [
        x[:, (part * 2 + half) * 16 : (part * 2 + half + 1) * 16, :].reshape(GRID, 128)
        for half in range(2)
    ]
    return jnp.concatenate(halves, axis=1)


def period_one(own, received, c, slot):
    piece = received[4 + 2 * slot + jnp.minimum(c, 1)]
    piece = jnp.concatenate([piece[:8], piece[8:]], axis=1)
    return jnp.where(c < 2, piece, own[slot])


def period_two(own, received, c, slot):
    piece = received[4 + 2 * slot + 1]
    piece = jnp.concatenate([piece[:8], piece[8:]], axis=1)
    return jnp.where(c < 1, piece, own[slot + 3])


def wake_sums(g, charges, rate, freq, amp, extra):
    source = lax.broadcasted_iota(jnp.int32, (8, 128), 1)
    pole = lax.broadcasted_iota(jnp.int32, (8, 128), 0)
    rates, freqs, amps = (jnp.zeros((8, 128), f32) for _ in range(3))
    for k in range(8):
        rates = jnp.where(pole == k, rate[k], rates)
        freqs = jnp.where(pole == k, freq[k], freqs)
        amps = jnp.where(pole == k, amp[k], amps)

    def total(value):
        return jnp.sum(jnp.sum(value, axis=0, keepdims=True), axis=1, keepdims=True)

    for k, back in enumerate((2, 1)):
        s = (g + SLICES - back) % SLICES
        steps = jnp.maximum(s - source, 0).astype(f32)
        power = jnp.exp(-rates * steps) * jnp.cos(freqs * steps)
        reach = jnp.where(source < s, power, jnp.where(source == s, 0.5, 0.0))
        wake = wake_gain / SLICES * total(amps * reach * charges)
        norm = total(jnp.where((source == s) & (pole == 0), charges, 0.0))
        extra[k] = jnp.broadcast_to(wake, (8, 128))
        extra[2 + k] = jnp.broadcast_to(norm, (8, 128))


def first_body(x, own, received, charges, rate, freq, amp, states, extra, re, im):
    b, _, c, _ = place()
    wake_sums(4 * b + c, charges[...], rate, freq, amp, extra)
    take = functools.partial(period_one, own, received, c)
    fr, fi = whole_field(x, 0), whole_field(x, 1)
    probe(fr, fi, take(2), take(3), re, im)
    angles = take(0)
    energies = (
        take(1)
        - kick_gain * (re[...] * jnp.cos(angles) - im[...] * jnp.sin(angles))
        - extra[0, 0:1, 0:1]
    )
    states[0] = angles + energies
    states[1] = energies


def second_body(x, states, own, received, extra, tall, field, re, im, again):
    again[...] = tall[...]
    b, _, c, _ = place()
    take = functools.partial(period_one, own, received, c)
    br, bi = deposit(states[0], take(4), take(2), take(3))
    strength = deposit_gain * extra[2, 0:1, 0:1]
    fr = deposited(whole_field(x, 0), br, strength)
    fi = deposited(whole_field(x, 1), bi, strength)
    fr, fi = times_right(fr, fi, tall[0], tall[1])
    fr, fi = times_left(tall[0], tall[1], fr, fi)
    first = (b == 0) & (c == 1)
    fr = jnp.where(first, 0.0, fr)
    fi = jnp.where(first, 0.0, fi)
    field[0] = fr
    field[1] = fi
    take = functools.partial(period_two, own, received, c)
    probe(fr, fi, take(2), take(3), re, im)


def third_body(states, extra, re, im, out):
    angles = states[0]
    energies = (
        states[1]
        - kick_gain * (re[...] * jnp.cos(angles) - im[...] * jnp.sin(angles))
        - extra[1, 0:1, 0:1]
    )
    out[0] = angles + energies
    out[1] = energies


def fourth_body(field, states, own, received, extra, tall, out):
    b, _, c, r = place()
    take = functools.partial(period_two, own, received, c)
    br, bi = deposit(states[0], take(4), take(2), take(3))
    strength = deposit_gain * extra[3, 0:1, 0:1]
    fr = deposited(field[0], br, strength)
    fi = deposited(field[1], bi, strength)
    at = pl.multiple_of(r * 64, 64)
    ah, al = (
        jnp.concatenate([tall[k, pl.ds(at, 64), :], tall[k, pl.ds(GRID + at, 64), :]], axis=0)
        for k in range(2)
    )
    fr, fi = times_left(ah, al, fr, fi)
    fr, fi = times_right(fr, fi, tall[0], tall[1])
    empty = (b == 0) & (c == 0)
    for part, value in enumerate((fr, fi)):
        value = jnp.where(empty, 0.0, value)
        for j in range(4):
            out[j, part * 16 : part * 16 + 16, :] = value[16 * j : 16 * j + 16]


def last_body(x, field, phase, energy):
    for c in range(4):
        for part in range(2):
            field[part, c] = x[c, part * 16 : part * 16 + 16, :]
        for k, target in enumerate((phase, energy)):
            for half in range(2):
                at = 32 + (k * 2 + half) * 8
                piece = x[c, at : at + 8, :]
                for q in range(ROWS):
                    begin = q * WIDE + half * 256
                    target[c : c + 1, begin : begin + 256] = piece[q : q + 1]


def call(body, outs, *args, scalars=(), plain=(), last=False, room=0):
    specs, inputs = [], []
    for k, arg in enumerate(args):
        specs.append(pl.BlockSpec(memory_space=pltpu.SMEM if k in scalars else pltpu.VMEM))
        if k not in scalars and k not in plain:
            arg = pltpu.with_memory_space_constraint(arg, pltpu.VMEM)
        inputs.append(arg)
    kind = jax.ShapeDtypeStruct if last else pltpu.VMEM
    return pl.pallas_call(
        body,
        out_shape=[kind(shape, bf16 if shape == TABLE else f32) for shape in outs],
        in_specs=specs,
        out_specs=[pl.BlockSpec(memory_space=pltpu.VMEM) for _ in outs],
        compiler_params=pltpu.CompilerParams(vmem_limit_bytes=room << 20) if room else None,
    )(*inputs)


def shards(
    field_in, phases, energy, row_cell, col_cell, weight, charge, pole_rate, pole_freq, pole_amp
):
    tall = jnp.asarray(propagation_table())
    kept = (8, ROWS, WIDE)
    state_shape = (2, ROWS, WIDE)
    line = (ROWS, WIDE)
    send, own, charges = call(
        prep_body,
        [(14, 16, GRID), kept, (1, SLICES)],
        field_in, phases, energy, row_cell, col_cell, weight, charge,
        scalars=(6,), plain=range(6),
    )
    received = lax.ppermute(send, "beam", NEXT_BEAM)
    charges = jnp.broadcast_to(charges[None], (BEAM, 1, SLICES))
    charges = lax.all_to_all(charges, "beam", 0, 0, tiled=True)
    charges = jnp.sum(charges, axis=0)
    (packed,) = call(pack_body, [(TRANS, 64, 128)], field_in, received)
    x = lax.all_to_all(packed, "trans", 0, 0, tiled=True)
    states, extra, _, _ = call(
        first_body,
        [state_shape, (4, 8, 128), line, line],
        x, own, received, charges, pole_rate, pole_freq, pole_amp,
        scalars=(4, 5, 6),
    )
    following = lax.ppermute(states, JOINT, TO_PREVIOUS)
    field, re, im, tall = call(
        second_body,
        [(2, GRID, GRID), line, line, TABLE],
        x, states, own, received, extra, tall, room=24,
    )
    (final,) = call(third_body, [state_shape], following, extra, re, im, room=24)
    home = lax.ppermute(final, JOINT, TO_PREVIOUS)
    (bands,) = call(
        fourth_body, [(4, 32, GRID)], field, final, own, received, extra, tall, room=24
    )
    home = jnp.concatenate([home[..., :256], home[..., 256:]], axis=1).reshape(32, 256)
    both = jnp.concatenate([bands, jnp.broadcast_to(home[None], (4, 32, 256))], axis=1)
    y = lax.all_to_all(both, "trans", 0, 0, tiled=True, axis_index_groups=QUADS)
    return tuple(
        call(last_body, [(2, 4, 16, GRID), (4, NPART), (4, NPART)], y, last=True)
    )


def solution(mesh):
    placed = (
        P(None, "beam", "trans", None),
        P("beam", None),
        P("beam", None),
        P("beam", None),
        P("beam", None),
        P("beam", None),
        P("beam"),
        P(),
        P(),
        P(),
    )
    return jax.shard_map(
        shards,
        mesh=mesh,
        in_specs=placed,
        out_specs=(P(None, "beam", "trans", None), P("beam", None), P("beam", None)),
        check_vma=False,
    )
```

```python
import functools

import jax
import jax.numpy as jnp
import numpy as np
from jax import lax
from jax.experimental import pallas as pl
from jax.experimental.pallas import tpu as pltpu
from jax.sharding import PartitionSpec as P

diffraction = 20.0
kick_gain = 0.5
deposit_gain = 0.05
wake_gain = 3.0
charge_unit = 1024.0

GRID = 256
SLICES = 128
NPART = 4096
BEAM = 32
TRANS = 16
LOW, HIGH = 32, 224
SPAN = HIGH - LOW
TABLE = (2, 2 * GRID, GRID)
ROWS, WIDE = 8, 512
JOINT = ("beam", "trans")
QUADS = [[4 * r + c for c in range(4)] for r in range(4)]

f32 = jnp.float32
bf16 = jnp.bfloat16


def propagation_table():
    n = np.arange(GRID)
    centred = ((n + GRID // 2) % GRID - GRID // 2) / GRID
    k = np.exp(-1j * diffraction * centred**2)
    h = np.fft.ifft(k)
    a = h[(n[:, None] - n[None, :]) % GRID]
    parts = np.stack([a.real, a.imag]).astype(np.float32)
    high = parts.astype(jnp.bfloat16)
    low = (parts - high.astype(np.float32)).astype(jnp.bfloat16)
    return np.stack([part.reshape(2 * GRID, GRID) for part in (high, low)])


def moved(fn):
    out = []
    for b in range(BEAM):
        for t in range(TRANS):
            b2, t2 = fn(b, t)
            out.append((b * TRANS + t, (b2 % BEAM) * TRANS + t2))
    return out


TO_PREVIOUS = moved(lambda b, t: ((4 * b + t % 4 - 1) // 4, t // 4 * 4 + (t % 4 - 1) % 4))
NEXT_BEAM = [(b, (b + 1) % BEAM) for b in range(BEAM)]


def split(x):
    high = x.astype(bf16)
    return high, (x - high.astype(f32)).astype(bf16)


def dot(a, b):
    return jnp.dot(a, b, preferred_element_type=f32)


def times_right(xr, xi, high, low):
    p = []
    for x in (xr, xi):
        xh, xl = split(x)
        for k in range(2):
            h, w = high[k * GRID : (k + 1) * GRID], low[k * GRID : (k + 1) * GRID]
            p.append(dot(xh, h) + dot(xl, h) + dot(xh, w))
    return p[0] - p[3], p[1] + p[2]


def times_left(ah, al, xr, xi):
    m = ah.shape[0] // 2
    xh, xl = split(jnp.concatenate([xr, xi], axis=1))
    q = []
    for k in range(2):
        high, low = ah[k * m : (k + 1) * m], al[k * m : (k + 1) * m]
        q.append(dot(high, xh) + dot(low, xh) + dot(high, xl))
    return q[0][:, :GRID] - q[1][:, GRID:], q[1][:, :GRID] + q[0][:, GRID:]


def iota_rows(first, count):
    return lax.broadcasted_iota(jnp.int32, (count, WIDE), 0).astype(f32) + float(first)


def hot(values, rows_bf):
    return jnp.where(rows_bf == values.astype(bf16), jnp.ones((), bf16), jnp.zeros((), bf16))


def probe(fr, fi, rows, cols, out_re, out_im):
    high, low = split(jnp.concatenate([fr[LOW:HIGH], fi[LOW:HIGH]], axis=0))
    col_iota = iota_rows(0, GRID).astype(bf16)
    offset = rows.astype(jnp.int32) - LOW
    inside = lax.broadcasted_iota(jnp.int32, (8, WIDE), 0)
    for q in range(ROWS):
        col_hot = hot(cols[q : q + 1], col_iota)
        found = dot(high, col_hot) + dot(low, col_hot)
        at = jnp.broadcast_to(offset[q : q + 1], (8, WIDE))
        group = at >> 3
        got_re, got_im = found[:8], found[SPAN : SPAN + 8]
        for k in range(1, SPAN // 8):
            here = group == k
            got_re = jnp.where(here, found[8 * k : 8 * k + 8], got_re)
            got_im = jnp.where(here, found[SPAN + 8 * k : SPAN + 8 * k + 8], got_im)
        mine = (at & 7) == inside
        out_re[q : q + 1, :] = jnp.sum(jnp.where(mine, got_re, 0.0), axis=0, keepdims=True)
        out_im[q : q + 1, :] = jnp.sum(jnp.where(mine, got_im, 0.0), axis=0, keepdims=True)


def deposit(angles, weights, rows, cols):
    v = (weights * jnp.cos(angles)).astype(bf16)
    u = (-weights * jnp.sin(angles)).astype(bf16)
    col_iota = iota_rows(0, GRID).astype(bf16)
    row_iota = iota_rows(LOW, SPAN).astype(bf16)
    zero = jnp.zeros((), bf16)
    total = [jnp.zeros((SPAN, GRID), f32)] * 2
    for q in range(ROWS):
        col_hot = hot(cols[q : q + 1], col_iota)
        mask = row_iota == rows[q : q + 1].astype(bf16)
        for k, value in enumerate((v, u)):
            left = jnp.where(mask, value[q : q + 1], zero)
            total[k] = total[k] + lax.dot_general(
                left, col_hot, (((1,), (1,)), ((), ())), preferred_element_type=f32
            )
    return total


def deposited(field, change, strength):
    return jnp.concatenate(
        [field[:LOW], field[LOW:HIGH] + strength * change, field[HIGH:]], axis=0
    )


def place():
    t = lax.axis_index("trans")
    return lax.axis_index("beam"), t, t % 4, t // 4


def prep_body(field, phases, energy, row, col, weight, charge, send, own, charges):
    b, _, c, _ = place()
    for part in range(2):
        for k in range(2):
            send[part * 2 + k] = field[part, 2 + k]
    own_one, own_two = jnp.maximum(c - 2, 0), jnp.maximum(c - 1, 0)

    def pick(ref, index, slot):
        line = ref[pl.ds(index, 1), :].astype(f32)
        for q in range(ROWS):
            own[slot, q : q + 1, :] = line[:, q * WIDE : (q + 1) * WIDE]

    for slot, ref in enumerate((phases, energy, row, col, weight)):
        pick(ref, own_one, slot)
        for k in range(2):
            line = ref[2 + k : 3 + k, :].astype(f32)
            for q in range(ROWS):
                for half in range(2):
                    begin = q * WIDE + half * 256
                    at = half * 8 + q
                    send[4 + 2 * slot + k, at : at + 1, :] = line[:, begin : begin + 256]
    for slot, ref in enumerate((row, col, weight)):
        pick(ref, own_two, 5 + slot)
    lane = lax.broadcasted_iota(jnp.int32, (1, SLICES), 1)
    line = jnp.zeros((1, SLICES), f32)
    for k in range(4):
        line = jnp.where(lane == 4 * b + k, charge[k].astype(f32) / charge_unit, line)
    charges[...] = line


def pack_body(field, received, out):
    for c in range(4):
        for part in range(2):
            piece = received[part * 2 + c] if c < 2 else field[part, c - 2]
            for half in range(2):
                at = (part * 2 + half) * 16
                for r in range(4):
                    out[4 * r + c, at : at + 16, :] = piece[:, half * 128 : (half + 1) * 128]


def whole_field(x, part):
    halves = [
        x[:, (part * 2 + half) * 16 : (part * 2 + half + 1) * 16, :].reshape(GRID, 128)
        for half in range(2)
    ]
    return jnp.concatenate(halves, axis=1)


def period_one(own, received, c, slot):
    piece = received[4 + 2 * slot + jnp.minimum(c, 1)]
    piece = jnp.concatenate([piece[:8], piece[8:]], axis=1)
    return jnp.where(c < 2, piece, own[slot])


def period_two(own, received, c, slot):
    piece = received[4 + 2 * slot + 1]
    piece = jnp.concatenate([piece[:8], piece[8:]], axis=1)
    return jnp.where(c < 1, piece, own[slot + 3])


def wake_sums(g, charges, rate, freq, amp, extra):
    source = lax.broadcasted_iota(jnp.int32, (8, 128), 1)
    pole = lax.broadcasted_iota(jnp.int32, (8, 128), 0)
    rates, freqs, amps = (jnp.zeros((8, 128), f32) for _ in range(3))
    for k in range(8):
        rates = jnp.where(pole == k, rate[k], rates)
        freqs = jnp.where(pole == k, freq[k], freqs)
        amps = jnp.where(pole == k, amp[k], amps)

    def total(value):
        return jnp.sum(jnp.sum(value, axis=0, keepdims=True), axis=1, keepdims=True)

    for k, back in enumerate((2, 1)):
        s = (g + SLICES - back) % SLICES
        steps = jnp.maximum(s - source, 0).astype(f32)
        power = jnp.exp(-rates * steps) * jnp.cos(freqs * steps)
        reach = jnp.where(source < s, power, jnp.where(source == s, 0.5, 0.0))
        wake = wake_gain / SLICES * total(amps * reach * charges)
        norm = total(jnp.where((source == s) & (pole == 0), charges, 0.0))
        extra[k] = jnp.broadcast_to(wake, (8, 128))
        extra[2 + k] = jnp.broadcast_to(norm, (8, 128))


def first_body(x, own, received, charges, rate, freq, amp, states, extra, re, im):
    b, _, c, _ = place()
    wake_sums(4 * b + c, charges[...], rate, freq, amp, extra)
    take = functools.partial(period_one, own, received, c)
    fr, fi = whole_field(x, 0), whole_field(x, 1)
    probe(fr, fi, take(2), take(3), re, im)
    angles = take(0)
    energies = (
        take(1)
        - kick_gain * (re[...] * jnp.cos(angles) - im[...] * jnp.sin(angles))
        - extra[0, 0:1, 0:1]
    )
    states[0] = angles + energies
    states[1] = energies


def second_body(x, states, own, received, extra, tall, field, re, im, again):
    again[...] = tall[...]
    b, _, c, _ = place()
    take = functools.partial(period_one, own, received, c)
    br, bi = deposit(states[0], take(4), take(2), take(3))
    strength = deposit_gain * extra[2, 0:1, 0:1]
    fr = deposited(whole_field(x, 0), br, strength)
    fi = deposited(whole_field(x, 1), bi, strength)
    fr, fi = times_right(fr, fi, tall[0], tall[1])
    fr, fi = times_left(tall[0], tall[1], fr, fi)
    first = (b == 0) & (c == 1)
    fr = jnp.where(first, 0.0, fr)
    fi = jnp.where(first, 0.0, fi)
    field[0] = fr
    field[1] = fi
    take = functools.partial(period_two, own, received, c)
    probe(fr, fi, take(2), take(3), re, im)


def third_body(states, extra, re, im, out):
    angles = states[0]
    energies = (
        states[1]
        - kick_gain * (re[...] * jnp.cos(angles) - im[...] * jnp.sin(angles))
        - extra[1, 0:1, 0:1]
    )
    out[0] = angles + energies
    out[1] = energies


def fourth_body(field, states, own, received, extra, tall, out):
    b, _, c, r = place()
    take = functools.partial(period_two, own, received, c)
    br, bi = deposit(states[0], take(4), take(2), take(3))
    strength = deposit_gain * extra[3, 0:1, 0:1]
    fr = deposited(field[0], br, strength)
    fi = deposited(field[1], bi, strength)
    at = pl.multiple_of(r * 64, 64)
    ah, al = (
        jnp.concatenate([tall[k, pl.ds(at, 64), :], tall[k, pl.ds(GRID + at, 64), :]], axis=0)
        for k in range(2)
    )
    fr, fi = times_left(ah, al, fr, fi)
    fr, fi = times_right(fr, fi, tall[0], tall[1])
    empty = (b == 0) & (c == 0)
    for part, value in enumerate((fr, fi)):
        value = jnp.where(empty, 0.0, value)
        for j in range(4):
            out[j, part * 16 : part * 16 + 16, :] = value[16 * j : 16 * j + 16]


def last_body(x, field, phase, energy):
    for c in range(4):
        for part in range(2):
            field[part, c] = x[c, part * 16 : part * 16 + 16, :]
        for k, target in enumerate((phase, energy)):
            for half in range(2):
                at = 32 + (k * 2 + half) * 8
                piece = x[c, at : at + 8, :]
                for q in range(ROWS):
                    begin = q * WIDE + half * 256
                    target[c : c + 1, begin : begin + 256] = piece[q : q + 1]


def call(body, outs, *args, scalars=(), plain=(), last=False, room=0):
    specs, inputs = [], []
    for k, arg in enumerate(args):
        specs.append(pl.BlockSpec(memory_space=pltpu.SMEM if k in scalars else pltpu.VMEM))
        if k not in scalars and k not in plain:
            arg = pltpu.with_memory_space_constraint(arg, pltpu.VMEM)
        inputs.append(arg)
    kind = jax.ShapeDtypeStruct if last else pltpu.VMEM
    return pl.pallas_call(
        body,
        out_shape=[kind(shape, bf16 if shape == TABLE else f32) for shape in outs],
        in_specs=specs,
        out_specs=[pl.BlockSpec(memory_space=pltpu.VMEM) for _ in outs],
        compiler_params=pltpu.CompilerParams(vmem_limit_bytes=room << 20) if room else None,
    )(*inputs)


def shards(
    field_in, phases, energy, row_cell, col_cell, weight, charge, pole_rate, pole_freq, pole_amp
):
    tall = jnp.asarray(propagation_table())
    kept = (8, ROWS, WIDE)
    state_shape = (2, ROWS, WIDE)
    line = (ROWS, WIDE)
    send, own, charges = call(
        prep_body,
        [(14, 16, GRID), kept, (1, SLICES)],
        field_in, phases, energy, row_cell, col_cell, weight, charge,
        scalars=(6,), plain=range(6),
    )
    received = lax.ppermute(send, "beam", NEXT_BEAM)
    charges = jnp.broadcast_to(charges[None], (BEAM, 1, SLICES))
    charges = lax.all_to_all(charges, "beam", 0, 0, tiled=True)
    charges = jnp.sum(charges, axis=0)
    (packed,) = call(pack_body, [(TRANS, 64, 128)], field_in, received)
    x = lax.all_to_all(packed, "trans", 0, 0, tiled=True)
    states, extra, _, _ = call(
        first_body,
        [state_shape, (4, 8, 128), line, line],
        x, own, received, charges, pole_rate, pole_freq, pole_amp,
        scalars=(4, 5, 6),
    )
    following = lax.ppermute(states, JOINT, TO_PREVIOUS)
    field, re, im, tall = call(
        second_body,
        [(2, GRID, GRID), line, line, TABLE],
        x, states, own, received, extra, tall, room=24,
    )
    (final,) = call(third_body, [state_shape], following, extra, re, im, room=24)
    home = lax.ppermute(final, JOINT, TO_PREVIOUS)
    (bands,) = call(
        fourth_body, [(4, 32, GRID)], field, final, own, received, extra, tall, room=24
    )
    home = jnp.concatenate([home[..., :256], home[..., 256:]], axis=1).reshape(32, 256)
    both = jnp.concatenate([bands, jnp.broadcast_to(home[None], (4, 32, 256))], axis=1)
    y = lax.all_to_all(both, "trans", 0, 0, tiled=True, axis_index_groups=QUADS)
    return tuple(
        call(last_body, [(2, 4, 16, GRID), (4, NPART), (4, NPART)], y, last=True)
    )


def solution(mesh):
    placed = (
        P(None, "beam", "trans", None),
        P("beam", None),
        P("beam", None),
        P("beam", None),
        P("beam", None),
        P("beam", None),
        P("beam"),
        P(),
        P(),
        P(),
    )
    return jax.shard_map(
        shards,
        mesh=mesh,
        in_specs=placed,
        out_specs=(P(None, "beam", "trans", None), P("beam", None), P("beam", None)),
        check_vma=False,
    )
```

```python
import functools

import jax
import jax.numpy as jnp
import numpy as np
from jax import lax
from jax.experimental import pallas as pl
from jax.experimental.pallas import tpu as pltpu
from jax.sharding import PartitionSpec as P

diffraction = 20.0
kick_gain = 0.5
deposit_gain = 0.05
wake_gain = 3.0
charge_unit = 1024.0

GRID = 256
SLICES = 128
NPART = 4096
BEAM = 32
TRANS = 16
LOW, HIGH = 32, 224
SPAN = HIGH - LOW
TABLE = (2, 2 * GRID, GRID)
ROWS, WIDE = 8, 512
JOINT = ("beam", "trans")
QUADS = [[4 * r + c for c in range(4)] for r in range(4)]

f32 = jnp.float32
bf16 = jnp.bfloat16


def propagation_table():
    n = np.arange(GRID)
    centred = ((n + GRID // 2) % GRID - GRID // 2) / GRID
    k = np.exp(-1j * diffraction * centred**2)
    h = np.fft.ifft(k)
    a = h[(n[:, None] - n[None, :]) % GRID]
    parts = np.stack([a.real, a.imag]).astype(np.float32)
    high = parts.astype(jnp.bfloat16)
    low = (parts - high.astype(np.float32)).astype(jnp.bfloat16)
    return np.stack([part.reshape(2 * GRID, GRID) for part in (high, low)])


def moved(fn):
    out = []
    for b in range(BEAM):
        for t in range(TRANS):
            b2, t2 = fn(b, t)
            out.append((b * TRANS + t, (b2 % BEAM) * TRANS + t2))
    return out


TO_PREVIOUS = moved(lambda b, t: ((4 * b + t % 4 - 1) // 4, t // 4 * 4 + (t % 4 - 1) % 4))
NEXT_BEAM = [(b, (b + 1) % BEAM) for b in range(BEAM)]


def split(x):
    high = x.astype(bf16)
    return high, (x - high.astype(f32)).astype(bf16)


def dot(a, b):
    return jnp.dot(a, b, preferred_element_type=f32)


def times_right(xr, xi, high, low):
    p = []
    for x in (xr, xi):
        xh, xl = split(x)
        for k in range(2):
            h, w = high[k * GRID : (k + 1) * GRID], low[k * GRID : (k + 1) * GRID]
            p.append(dot(xh, h) + dot(xl, h) + dot(xh, w))
    return p[0] - p[3], p[1] + p[2]


def times_left(ah, al, xr, xi):
    m = ah.shape[0] // 2
    xh, xl = split(jnp.concatenate([xr, xi], axis=1))
    q = []
    for k in range(2):
        high, low = ah[k * m : (k + 1) * m], al[k * m : (k + 1) * m]
        q.append(dot(high, xh) + dot(low, xh) + dot(high, xl))
    return q[0][:, :GRID] - q[1][:, GRID:], q[1][:, :GRID] + q[0][:, GRID:]


def iota_rows(first, count):
    return lax.broadcasted_iota(jnp.int32, (count, WIDE), 0).astype(f32) + float(first)


def hot(values, rows_bf):
    return jnp.where(rows_bf == values.astype(bf16), jnp.ones((), bf16), jnp.zeros((), bf16))


def probe(fr, fi, rows, cols, out_re, out_im):
    high, low = split(jnp.concatenate([fr[LOW:HIGH], fi[LOW:HIGH]], axis=0))
    col_iota = iota_rows(0, GRID).astype(bf16)
    offset = rows.astype(jnp.int32) - LOW
    inside = lax.broadcasted_iota(jnp.int32, (8, WIDE), 0)
    for q in range(ROWS):
        col_hot = hot(cols[q : q + 1], col_iota)
        found = dot(high, col_hot) + dot(low, col_hot)
        at = jnp.broadcast_to(offset[q : q + 1], (8, WIDE))
        group = at >> 3
        got_re, got_im = found[:8], found[SPAN : SPAN + 8]
        for k in range(1, SPAN // 8):
            here = group == k
            got_re = jnp.where(here, found[8 * k : 8 * k + 8], got_re)
            got_im = jnp.where(here, found[SPAN + 8 * k : SPAN + 8 * k + 8], got_im)
        mine = (at & 7) == inside
        out_re[q : q + 1, :] = jnp.sum(jnp.where(mine, got_re, 0.0), axis=0, keepdims=True)
        out_im[q : q + 1, :] = jnp.sum(jnp.where(mine, got_im, 0.0), axis=0, keepdims=True)


def deposit(angles, weights, rows, cols):
    v = (weights * jnp.cos(angles)).astype(bf16)
    u = (-weights * jnp.sin(angles)).astype(bf16)
    col_iota = iota_rows(0, GRID).astype(bf16)
    row_iota = iota_rows(LOW, SPAN).astype(bf16)
    zero = jnp.zeros((), bf16)
    total = [jnp.zeros((SPAN, GRID), f32)] * 2
    for q in range(ROWS):
        col_hot = hot(cols[q : q + 1], col_iota)
        mask = row_iota == rows[q : q + 1].astype(bf16)
        for k, value in enumerate((v, u)):
            left = jnp.where(mask, value[q : q + 1], zero)
            total[k] = total[k] + lax.dot_general(
                left, col_hot, (((1,), (1,)), ((), ())), preferred_element_type=f32
            )
    return total


def deposited(field, change, strength):
    return jnp.concatenate(
        [field[:LOW], field[LOW:HIGH] + strength * change, field[HIGH:]], axis=0
    )


def place():
    t = lax.axis_index("trans")
    return lax.axis_index("beam"), t, t % 4, t // 4


def prep_body(field, phases, energy, row, col, weight, charge, send, own, charges):
    b, _, c, _ = place()
    for part in range(2):
        for k in range(2):
            send[part * 2 + k] = field[part, 2 + k]
    own_one, own_two = jnp.maximum(c - 2, 0), jnp.maximum(c - 1, 0)

    def pick(ref, index, slot):
        line = ref[pl.ds(index, 1), :].astype(f32)
        for q in range(ROWS):
            own[slot, q : q + 1, :] = line[:, q * WIDE : (q + 1) * WIDE]

    for slot, ref in enumerate((phases, energy, row, col, weight)):
        pick(ref, own_one, slot)
        for k in range(2):
            line = ref[2 + k : 3 + k, :].astype(f32)
            for q in range(ROWS):
                for half in range(2):
                    begin = q * WIDE + half * 256
                    at = half * 8 + q
                    send[4 + 2 * slot + k, at : at + 1, :] = line[:, begin : begin + 256]
    for slot, ref in enumerate((row, col, weight)):
        pick(ref, own_two, 5 + slot)
    lane = lax.broadcasted_iota(jnp.int32, (1, SLICES), 1)
    line = jnp.zeros((1, SLICES), f32)
    for k in range(4):
        line = jnp.where(lane == 4 * b + k, charge[k].astype(f32) / charge_unit, line)
    charges[...] = line


def pack_body(field, received, out):
    for c in range(4):
        for part in range(2):
            piece = received[part * 2 + c] if c < 2 else field[part, c - 2]
            for half in range(2):
                at = (part * 2 + half) * 16
                for r in range(4):
                    out[4 * r + c, at : at + 16, :] = piece[:, half * 128 : (half + 1) * 128]


def whole_field(x, part):
    halves = [
        x[:, (part * 2 + half) * 16 : (part * 2 + half + 1) * 16, :].reshape(GRID, 128)
        for half in range(2)
    ]
    return jnp.concatenate(halves, axis=1)


def period_one(own, received, c, slot):
    piece = received[4 + 2 * slot + jnp.minimum(c, 1)]
    piece = jnp.concatenate([piece[:8], piece[8:]], axis=1)
    return jnp.where(c < 2, piece, own[slot])


def period_two(own, received, c, slot):
    piece = received[4 + 2 * slot + 1]
    piece = jnp.concatenate([piece[:8], piece[8:]], axis=1)
    return jnp.where(c < 1, piece, own[slot + 3])


def wake_sums(g, charges, rate, freq, amp, extra):
    source = lax.broadcasted_iota(jnp.int32, (8, 128), 1)
    pole = lax.broadcasted_iota(jnp.int32, (8, 128), 0)
    rates, freqs, amps = (jnp.zeros((8, 128), f32) for _ in range(3))
    for k in range(8):
        rates = jnp.where(pole == k, rate[k], rates)
        freqs = jnp.where(pole == k, freq[k], freqs)
        amps = jnp.where(pole == k, amp[k], amps)

    def total(value):
        return jnp.sum(jnp.sum(value, axis=0, keepdims=True), axis=1, keepdims=True)

    for k, back in enumerate((2, 1)):
        s = (g + SLICES - back) % SLICES
        steps = jnp.maximum(s - source, 0).astype(f32)
        power = jnp.exp(-rates * steps) * jnp.cos(freqs * steps)
        reach = jnp.where(source < s, power, jnp.where(source == s, 0.5, 0.0))
        wake = wake_gain / SLICES * total(amps * reach * charges)
        norm = total(jnp.where((source == s) & (pole == 0), charges, 0.0))
        extra[k] = jnp.broadcast_to(wake, (8, 128))
        extra[2 + k] = jnp.broadcast_to(norm, (8, 128))


def first_body(x, own, received, charges, rate, freq, amp, states, extra, re, im):
    b, _, c, _ = place()
    wake_sums(4 * b + c, charges[...], rate, freq, amp, extra)
    take = functools.partial(period_one, own, received, c)
    fr, fi = whole_field(x, 0), whole_field(x, 1)
    probe(fr, fi, take(2), take(3), re, im)
    angles = take(0)
    energies = (
        take(1)
        - kick_gain * (re[...] * jnp.cos(angles) - im[...] * jnp.sin(angles))
        - extra[0, 0:1, 0:1]
    )
    states[0] = angles + energies
    states[1] = energies


def second_body(x, states, own, received, extra, tall, field, re, im, again):
    again[...] = tall[...]
    b, _, c, _ = place()
    take = functools.partial(period_one, own, received, c)
    br, bi = deposit(states[0], take(4), take(2), take(3))
    strength = deposit_gain * extra[2, 0:1, 0:1]
    fr = deposited(whole_field(x, 0), br, strength)
    fi = deposited(whole_field(x, 1), bi, strength)
    fr, fi = times_right(fr, fi, tall[0], tall[1])
    fr, fi = times_left(tall[0], tall[1], fr, fi)
    first = (b == 0) & (c == 1)
    fr = jnp.where(first, 0.0, fr)
    fi = jnp.where(first, 0.0, fi)
    field[0] = fr
    field[1] = fi
    take = functools.partial(period_two, own, received, c)
    probe(fr, fi, take(2), take(3), re, im)


def third_body(states, extra, re, im, out, lines):
    angles = states[0]
    energies = (
        states[1]
        - kick_gain * (re[...] * jnp.cos(angles) - im[...] * jnp.sin(angles))
        - extra[1, 0:1, 0:1]
    )
    for k, value in enumerate((angles + energies, energies)):
        out[k] = value
        for half in range(2):
            at = (k * 2 + half) * 8
            lines[at : at + 8, :] = value[:, half * 256 : half * 256 + 256]


def fourth_body(field, states, own, received, extra, tall, out):
    b, _, c, r = place()
    take = functools.partial(period_two, own, received, c)
    br, bi = deposit(states[0], take(4), take(2), take(3))
    strength = deposit_gain * extra[3, 0:1, 0:1]
    fr = deposited(field[0], br, strength)
    fi = deposited(field[1], bi, strength)
    at = pl.multiple_of(r * 64, 64)
    ah, al = (
        jnp.concatenate([tall[k, pl.ds(at, 64), :], tall[k, pl.ds(GRID + at, 64), :]], axis=0)
        for k in range(2)
    )
    fr, fi = times_left(ah, al, fr, fi)
    fr, fi = times_right(fr, fi, tall[0], tall[1])
    empty = (b == 0) & (c == 0)
    for part, value in enumerate((fr, fi)):
        value = jnp.where(empty, 0.0, value)
        for j in range(4):
            out[j, part * 16 : part * 16 + 16, :] = value[16 * j : 16 * j + 16]


def last_body(x, field, phase, energy):
    for c in range(4):
        for part in range(2):
            field[part, c] = x[c, part * 16 : part * 16 + 16, :]
        for k, target in enumerate((phase, energy)):
            for half in range(2):
                at = 32 + (k * 2 + half) * 8
                piece = x[c, at : at + 8, :]
                for q in range(ROWS):
                    begin = q * WIDE + half * 256
                    target[c : c + 1, begin : begin + 256] = piece[q : q + 1]


def call(body, outs, *args, scalars=(), plain=(), last=False, room=0):
    specs, inputs = [], []
    for k, arg in enumerate(args):
        specs.append(pl.BlockSpec(memory_space=pltpu.SMEM if k in scalars else pltpu.VMEM))
        if k not in scalars and k not in plain:
            arg = pltpu.with_memory_space_constraint(arg, pltpu.VMEM)
        inputs.append(arg)
    kind = jax.ShapeDtypeStruct if last else pltpu.VMEM
    return pl.pallas_call(
        body,
        out_shape=[kind(shape, bf16 if shape == TABLE else f32) for shape in outs],
        in_specs=specs,
        out_specs=[pl.BlockSpec(memory_space=pltpu.VMEM) for _ in outs],
        compiler_params=pltpu.CompilerParams(vmem_limit_bytes=room << 20) if room else None,
    )(*inputs)


def shards(
    field_in, phases, energy, row_cell, col_cell, weight, charge, pole_rate, pole_freq, pole_amp
):
    tall = jnp.asarray(propagation_table())
    kept = (8, ROWS, WIDE)
    state_shape = (2, ROWS, WIDE)
    line = (ROWS, WIDE)
    send, own, charges = call(
        prep_body,
        [(14, 16, GRID), kept, (1, SLICES)],
        field_in, phases, energy, row_cell, col_cell, weight, charge,
        scalars=(6,), plain=range(6),
    )
    received = lax.ppermute(send, "beam", NEXT_BEAM)
    charges = jnp.broadcast_to(charges[None], (BEAM, 1, SLICES))
    charges = lax.all_to_all(charges, "beam", 0, 0, tiled=True)
    charges = jnp.sum(charges, axis=0)
    (packed,) = call(pack_body, [(TRANS, 64, 128)], field_in, received)
    x = lax.all_to_all(packed, "trans", 0, 0, tiled=True)
    states, extra, _, _ = call(
        first_body,
        [state_shape, (4, 8, 128), line, line],
        x, own, received, charges, pole_rate, pole_freq, pole_amp,
        scalars=(4, 5, 6),
    )
    following = lax.ppermute(states, JOINT, TO_PREVIOUS)
    field, re, im, tall = call(
        second_body,
        [(2, GRID, GRID), line, line, TABLE],
        x, states, own, received, extra, tall, room=24,
    )
    final, lines = call(
        third_body, [state_shape, (32, 256)], following, extra, re, im, room=24
    )
    home = lax.ppermute(lines, JOINT, TO_PREVIOUS)
    (bands,) = call(
        fourth_body, [(4, 32, GRID)], field, final, own, received, extra, tall, room=24
    )
    both = jnp.concatenate([bands, jnp.broadcast_to(home[None], (4, 32, 256))], axis=1)
    y = lax.all_to_all(both, "trans", 0, 0, tiled=True, axis_index_groups=QUADS)
    return tuple(
        call(last_body, [(2, 4, 16, GRID), (4, NPART), (4, NPART)], y, last=True)
    )


def solution(mesh):
    placed = (
        P(None, "beam", "trans", None),
        P("beam", None),
        P("beam", None),
        P("beam", None),
        P("beam", None),
        P("beam", None),
        P("beam"),
        P(),
        P(),
        P(),
    )
    return jax.shard_map(
        shards,
        mesh=mesh,
        in_specs=placed,
        out_specs=(P(None, "beam", "trans", None), P("beam", None), P("beam", None)),
        check_vma=False,
    )
```
